32 devices in a mesh: dp: 8 (over z, x), tensor: 4 (over y, core).
Axes of the slice: x: 2, y: 2, z: 4, core: 2. Of those that a mesh axis runs over, the one named last changes fastest.
Arguments:
- inputs: bfloat16 [16, 1024, 768], P('dp'), may hold values from -6 to 6
- cotangent: bfloat16 [16, 1024, 768], P('dp'), may hold values from -6 to 6
- lengths: int32 [16], P('dp'), may hold values from 256 to 1024, as said below
- norm_gain: float32 [768], replicated, may hold values from 0.5 to 1.5
- norm_bias: float32 [768], replicated, may hold values from -2 to 2
- value_weight: bfloat16 [768, 3072], P('dp', 'tensor'), may hold values from -0.21875 to 0.21875
- value_bias: float32 [3072], P('tensor'), may hold values from -2 to 2
- feed_weight: bfloat16 [768, 1536], P('dp', 'tensor'), may hold values from -0.21875 to 0.21875
- feed_bias: float32 [1536], P('tensor'), may hold values from -2 to 2
- mix_forward: bfloat16 [1536, 3072], P('tensor', 'dp'), may hold values from -0.15625 to 0.15625
- mix_backward: bfloat16 [1536, 3072], P('tensor', 'dp'), may hold values from -0.15625 to 0.15625
- mix_bias: float32 [3072], P('tensor'), may hold values from -2 to 2
- out_weight: bfloat16 [3072, 768], P('tensor', 'dp'), may hold values from -0.21875 to 0.21875
- out_bias: float32 [768], replicated, may hold values from -2 to 2
- state_delta: float32 [2, 1536], P(None, 'tensor'), may hold values from -6 to -3
- state_rate: float32 [2, 1536, 64], P(None, 'tensor'), may hold values from 0.1 to 1
- state_readout: float32 [2, 1536, 64], P(None, 'tensor'), may hold values from -0.6 to 0.6
- state_skip: float32 [2, 1536], P(None, 'tensor'), may hold values from -3 to 3
Outputs:
- layer_out: bfloat16 [16, 1024, 768], P('dp')
- input_grad: bfloat16 [16, 1024, 768], P('dp')
- grad_norm_gain: float32 [768], replicated
- grad_norm_bias: float32 [768], replicated
- grad_value_weight: float32 [768, 3072], P('dp', 'tensor')
- grad_value_bias: float32 [3072], P('tensor')
- grad_feed_weight: float32 [768, 1536], P('dp', 'tensor')
- grad_feed_bias: float32 [1536], P('tensor')
- grad_mix_forward: float32 [1536, 3072], P('tensor', 'dp')
- grad_mix_backward: float32 [1536, 3072], P('tensor', 'dp')
- grad_mix_bias: float32 [3072], P('tensor')
- grad_out_weight: float32 [3072, 768], P('tensor', 'dp')
- grad_out_bias: float32 [768], replicated
- grad_state_delta: float32 [2, 1536], P(None, 'tensor')
- grad_state_rate: float32 [2, 1536, 64], P(None, 'tensor')
- grad_state_readout: float32 [2, 1536, 64], P(None, 'tensor')
- grad_state_skip: float32 [2, 1536], P(None, 'tensor')
The draws below stay inside these ranges and needn't reach their ends.
Inputs may be any that keep to these rules, and one draw needn't show every extreme that they name: `lengths`: each slot's number of valid positions; every draw has a slot of exactly 1024.
All inputs are finite; a program needn't handle non-finite values.
Results may differ from the reference program's by a relative error of at most 0.0067.
Values may be sent and summed in bfloat16 or wider, within the bound.
No kernel may reach another device: no remote copies, remote signals or barrier semaphores. Data moves between devices by JAX's collectives and lax.ppermute only.
A program may use at most 448 MiB of HBM per device.

```python
import math
import jax
import jax.numpy as jnp
from jax import lax

D = 768
HID = 3072
SSM = 1536
NST = 64
SEQ = 1024
SLOTS_ALL = 16


def draw_lengths(key, part):
    first_key, second_key = jax.random.split(jax.random.fold_in(key, 11))
    drawn = jax.random.randint(first_key, (SLOTS_ALL,), SEQ // 4, SEQ + 1)
    full_slot = jax.random.randint(second_key, (), 0, SLOTS_ALL)
    return jnp.where(jnp.arange(SLOTS_ALL) == full_slot, SEQ, drawn).astype(jnp.int32)


def levels(own_key, dims, shards, low, largest):
    def one(axis_at, blocks):
        heights = jax.random.uniform(jax.random.fold_in(jax.random.fold_in(own_key, 6), axis_at), (blocks,), jnp.float32, low / len(shards), largest / len(shards))
        return jnp.repeat(jnp.exp(heights), dims[axis_at] // blocks).reshape((-1,) + (1,) * (len(dims) - axis_at - 1))

    gain = one(*shards[0])
    for cut in shards[1:]:
        gain = gain * one(*cut)
    return gain


def gaussian(own_key, dims, width, limit, pieces=(), kind=jnp.bfloat16):
    entries = jax.random.normal(own_key, dims, jnp.float32) * width
    if len(pieces) > 0:
        entries = levels(own_key, dims, pieces, -0.22, 0.18) * entries
    return jnp.clip(entries, min=-limit, max=limit).astype(kind)


def setup_inputs(seed: int = 0) -> dict:
    seeds = jax.random.split(jax.random.key(seed), 19)
    inputs = gaussian(seeds[0], (SLOTS_ALL, SEQ, D), 1.0, 6.0, ((0, 8),))
    cotangent = gaussian(seeds[1], (SLOTS_ALL, SEQ, D), 1.0, 6.0, ((0, 8),))
    lengths = draw_lengths(jax.random.fold_in(seeds[18], 71), 0)
    norm_gain = jnp.clip(1.0 + 0.1 * jax.random.normal(seeds[3], (D,), jnp.float32), 0.5, 1.5)
    norm_bias = gaussian(seeds[4], (D,), 0.3, 2.0, (), jnp.float32)
    value_weight = gaussian(seeds[5], (D, HID), D ** -0.5, 0.21875, ((0, 8), (1, 4)))
    value_bias = gaussian(seeds[6], (HID,), 0.3, 2.0, ((0, 4),), jnp.float32)
    feed_weight = gaussian(seeds[7], (D, SSM), D ** -0.5, 0.21875, ((0, 8), (1, 4)))
    feed_bias = gaussian(seeds[8], (SSM,), 0.3, 2.0, ((0, 4),), jnp.float32)
    mix_forward = gaussian(seeds[9], (SSM, HID), SSM ** -0.5, 0.15625, ((0, 4), (1, 8)))
    mix_backward = gaussian(seeds[10], (SSM, HID), SSM ** -0.5, 0.15625, ((0, 4), (1, 8)))
    mix_bias = gaussian(seeds[11], (HID,), 0.3, 2.0, ((0, 4),), jnp.float32)
    out_weight = gaussian(seeds[12], (HID, D), (HID // 4) ** -0.5, 0.21875, ((0, 4), (1, 8)))
    out_bias = gaussian(seeds[13], (D,), 0.3, 2.0, (), jnp.float32)
    state_delta = jnp.clip(-6.0 + 3.0 * jax.random.uniform(seeds[14], (2, SSM), jnp.float32) ** levels(seeds[14], (2, SSM), ((1, 4),), -0.2, 0.2), -6.0, -3.0)
    state_rate = jnp.clip(jnp.exp(math.log(1.0) - 2.3025851 * jax.random.uniform(seeds[15], (2, SSM, NST), jnp.float32) ** levels(seeds[15], (2, SSM, NST), ((1, 4),), -0.2, 0.2)), 0.1, 1.0)
    state_readout = gaussian(seeds[16], (2, SSM, NST), 0.1, 0.6, ((1, 4),), jnp.float32)
    state_skip = gaussian(seeds[17], (2, SSM), 0.5, 3.0, ((1, 4),), jnp.float32)
    return {"inputs": inputs, "cotangent": cotangent, "lengths": lengths, "norm_gain": norm_gain, "norm_bias": norm_bias, "value_weight": value_weight, "value_bias": value_bias, "feed_weight": feed_weight, "feed_bias": feed_bias, "mix_forward": mix_forward, "mix_backward": mix_backward, "mix_bias": mix_bias, "out_weight": out_weight, "out_bias": out_bias, "state_delta": state_delta, "state_rate": state_rate, "state_readout": state_readout, "state_skip": state_skip}


EPSILON = 1e-05
PRECISE = lax.Precision.HIGHEST

@jax.custom_vjp
def low(v):
    return lax.optimization_barrier(v.astype(jnp.bfloat16)).astype(jnp.float32)

@jax.custom_vjp
def low_back(v):
    return v

def low_keep(v):
    return (low(v), None)

def low_pass(kept, grad):
    return (grad,)

def back_keep(v):
    return (v, None)

def back_low(kept, grad):
    return (low(grad),)
low.defvjp(low_keep, low_pass)
low_back.defvjp(back_keep, back_low)

def layer_norm(rows, norm_gain, norm_bias):
    center = rows - lax.optimization_barrier(jnp.mean(rows, axis=-1, keepdims=True))
    spread = lax.optimization_barrier(jnp.mean(center * center, axis=-1, keepdims=True))
    return center * lax.rsqrt(spread + EPSILON) * norm_gain + norm_bias

def matmul(left, right):
    return jnp.einsum('gsd,dh->gsh', left, right, precision=PRECISE)

def kernel_block(packed):
    log_step, decay_rate, readout = packed
    step_size = jnp.exp(log_step)[..., None]
    offsets = jnp.arange(SEQ, dtype=jnp.float32)
    powers = jnp.exp(-(step_size * decay_rate)[..., None] * offsets)
    return jnp.einsum('chn,chnk->chk', readout * step_size, powers, precision=PRECISE)

def kernels(log_step, decay_rate, readout):
    group_size = math.gcd(SSM, 128)
    group_count = SSM // group_size
    packed = (log_step.reshape(2, group_count, group_size).transpose(1, 0, 2), decay_rate.reshape(2, group_count, group_size, NST).transpose(1, 0, 2, 3), readout.reshape(2, group_count, group_size, NST).transpose(1, 0, 2, 3))
    result = lax.map(jax.checkpoint(kernel_block), packed)
    return result.transpose(1, 0, 2, 3).reshape(2, SSM, SEQ)

def convolve(signal, kernel):
    padded_size = 2 * SEQ
    spectrum = jnp.fft.rfft(signal, n=padded_size, axis=1) * jnp.fft.rfft(kernel.T, n=padded_size, axis=0)[None]
    return jnp.fft.irfft(spectrum, n=padded_size, axis=1)[:, :SEQ]

def layer_block(params, kernel_pair, rows_in, slot_lengths):
    norm_gain, norm_bias, value_weight, value_bias, feed_weight, feed_bias, mix_forward, mix_backward, mix_bias, out_weight, out_bias, state_delta, state_rate, state_readout, state_skip = params
    live_mask = (jnp.arange(SEQ)[None, :] < slot_lengths[:, None]).astype(jnp.float32)[:, :, None]
    normed = low(layer_norm(rows_in, norm_gain, norm_bias))
    value_act = jax.nn.gelu(low_back(matmul(normed, value_weight) + value_bias))
    signal = jax.nn.gelu(low_back(matmul(normed, feed_weight) + feed_bias)) * live_mask
    ahead_scan = low(convolve(signal, kernel_pair[0]) + state_skip[0] * signal)
    behind = low(jnp.flip(convolve(jnp.flip(signal, 1), kernel_pair[1]), 1) + state_skip[1] * signal)
    gate_act = jax.nn.gelu(low_back(matmul(ahead_scan, mix_forward) + matmul(behind, mix_backward) + mix_bias))
    hidden = low(gate_act * value_act)
    return live_mask * (rows_in + matmul(hidden, out_weight) + out_bias)

def reference(inputs, cotangent, lengths, norm_gain, norm_bias, value_weight, value_bias, feed_weight, feed_bias, mix_forward, mix_backward, mix_bias, out_weight, out_bias, state_delta, state_rate, state_readout, state_skip):
    params = (norm_gain.astype(jnp.float32), norm_bias.astype(jnp.float32), value_weight.astype(jnp.float32), value_bias.astype(jnp.float32), feed_weight.astype(jnp.float32), feed_bias.astype(jnp.float32), mix_forward.astype(jnp.float32), mix_backward.astype(jnp.float32), mix_bias.astype(jnp.float32), out_weight.astype(jnp.float32), out_bias.astype(jnp.float32), state_delta.astype(jnp.float32), state_rate.astype(jnp.float32), state_readout.astype(jnp.float32), state_skip.astype(jnp.float32))
    group = math.gcd(SLOTS_ALL, max(1, 4096 // SEQ))
    checked_block = jax.checkpoint(layer_block)

    def forward(params, rows_all):
        kernel_pair = kernels(params[11], params[12], params[13])

        def one_group(packed):
            return checked_block(params, kernel_pair, packed[0], packed[1])
        grouped = rows_all.reshape(SLOTS_ALL // group, group, SEQ, D)
        grouped_lengths = lengths.reshape(SLOTS_ALL // group, group)
        result = lax.map(one_group, (grouped, grouped_lengths))
        return result.reshape(SLOTS_ALL, SEQ, D)
    layer_out, pullback = jax.vjp(forward, params, inputs.astype(jnp.float32))
    param_grads, input_grad = pullback(cotangent.astype(jnp.float32))
    return (layer_out.astype(jnp.bfloat16), input_grad.astype(jnp.bfloat16), param_grads[0], param_grads[1], param_grads[2], param_grads[3], param_grads[4], param_grads[5], param_grads[6], param_grads[7], param_grads[8], param_grads[9], param_grads[10], param_grads[11], param_grads[12], param_grads[13], param_grads[14])
```

```python
import math

import jax
import jax.numpy as jnp
from jax import lax
from jax.experimental import pallas as pl
from jax.experimental.pallas import tpu as pltpu
from jax.sharding import PartitionSpec as P

EPSILON = 1e-05
LANES = 128
INNER = 32
BF = jnp.bfloat16
F32 = jnp.float32
GELU_C = math.sqrt(2.0 / math.pi)
GELU_A = 0.044715


def gelu_pair(x):
    square = x * x
    bend = jnp.tanh(GELU_C * x * (1.0 + GELU_A * square))
    half = 0.5 * (1.0 + bend)
    slope = half + 0.5 * x * (1.0 - bend * bend) * (GELU_C * (1.0 + 3.0 * GELU_A * square))
    return x * half, slope


def dot_nt(a, b):
    return lax.dot_general(a, b, (((1,), (1,)), ((), ())), preferred_element_type=F32)


def dot_tn(a, b):
    return lax.dot_general(a, b, (((0,), (0,)), ((), ())), preferred_element_type=F32)


def dot_nn(a, b):
    return jnp.dot(a, b, preferred_element_type=F32)


def fill_powers(rate_ref, one_ref, many_ref, scale):
    states = rate_ref.shape[0]
    offset = lax.broadcasted_iota(jnp.int32, (INNER, LANES), 0).astype(F32)

    def body(n, _):
        row = rate_ref[pl.ds(n, 1), :]
        one_ref[n] = jnp.exp(-(row * offset))
        wide = jnp.exp(-(row * (offset * float(INNER))))
        if scale is not None:
            wide = wide * scale[pl.ds(n, 1), :]
        many_ref[n] = wide
        return 0

    lax.fori_loop(0, states, body, 0)


def impulse_kernel(delta_ref, rate_ref, readout_ref, out_ref, a_ref, w_ref, one_ref, many_ref):
    states = rate_ref.shape[1]
    length = out_ref.shape[0]
    step = jnp.exp(delta_ref[0])
    a_ref[...] = step * rate_ref[0]
    w_ref[...] = step * readout_ref[0]
    fill_powers(a_ref, one_ref, many_ref, w_ref)
    group = 8
    for start in range(0, length // INNER, group):

        def body(n, sums):
            base = one_ref[n]
            return tuple(
                total + many_ref[n, start + j : start + j + 1, :] * base
                for j, total in enumerate(sums)
            )

        sums = lax.fori_loop(
            0, states, body, tuple(jnp.zeros((INNER, LANES), F32) for _ in range(group))
        )
        for j, total in enumerate(sums):
            at = (start + j) * INNER
            out_ref[at : at + INNER, :] = total


def impulse(delta, rate, readout, length):
    dirs, states, channels = rate.shape
    lanes = channels // LANES
    spec = pl.BlockSpec((1, states, LANES), lambda c, j: (c, 0, j))
    return pl.pallas_call(
        impulse_kernel,
        name="impulse",
        grid=(dirs, lanes),
        in_specs=[pl.BlockSpec((1, 1, LANES), lambda c, j: (c, 0, j)), spec, spec],
        out_specs=pl.BlockSpec((length, LANES), lambda c, j: (0, c * lanes + j)),
        out_shape=jax.ShapeDtypeStruct((length, dirs * channels), F32),
        scratch_shapes=[
            pltpu.VMEM((states, LANES), F32),
            pltpu.VMEM((states, LANES), F32),
            pltpu.VMEM((states, INNER, LANES), F32),
            pltpu.VMEM((states, length // INNER, LANES), F32),
        ],
    )(delta, rate, readout)


def state_grad_kernel(
    delta_ref, rate_ref, readout_ref, grad_ref, gdelta_ref, grate_ref, greadout_ref, a_ref, one_ref, many_ref, g_ref, m_ref
):
    states = rate_ref.shape[1]
    length = grad_ref.shape[0]
    step = jnp.exp(delta_ref[0])
    a_ref[...] = step * rate_ref[0]
    fill_powers(a_ref, one_ref, many_ref, None)
    offset = lax.broadcasted_iota(jnp.int32, (INNER, LANES), 0).astype(F32)
    group = 4
    zero = jnp.zeros((INNER, LANES), F32)

    def body(i, _):
        sums = [zero] * group
        moments = [zero] * group
        for k in range(length // INNER - 1, -1, -1):
            block = grad_ref[k * INNER : (k + 1) * INNER, :]
            for j in range(group):
                sums[j] = sums[j] + many_ref[i * group + j, k : k + 1, :] * block
                if k > 0:
                    moments[j] = moments[j] + sums[j]
        for j in range(group):
            n = i * group + j
            base = one_ref[n]
            g_ref[pl.ds(n, 1), :] = jnp.sum(base * sums[j], axis=0, keepdims=True)
            m_ref[pl.ds(n, 1), :] = jnp.sum(
                base * (offset * sums[j] + float(INNER) * moments[j]), axis=0, keepdims=True
            )
        return 0

    lax.fori_loop(0, states // group, body, 0)
    rate = rate_ref[0]
    readout = readout_ref[0]
    grad_w = g_ref[...]
    grad_a = -(step * readout) * m_ref[...]
    greadout_ref[0] = step * grad_w
    grate_ref[0] = step * grad_a
    gdelta_ref[0] = step * jnp.sum(readout * grad_w + rate * grad_a, axis=0, keepdims=True)


def state_grad(delta, rate, readout, grad):
    dirs, states, channels = rate.shape
    length = grad.shape[0]
    lanes = channels // LANES
    spec = pl.BlockSpec((1, states, LANES), lambda c, j: (c, 0, j))
    row = pl.BlockSpec((1, 1, LANES), lambda c, j: (c, 0, j))
    return pl.pallas_call(
        state_grad_kernel,
        name="state_grad",
        grid=(dirs, lanes),
        in_specs=[row, spec, spec, pl.BlockSpec((length, LANES), lambda c, j: (0, c * lanes + j))],
        out_specs=[row, spec, spec],
        out_shape=[
            jax.ShapeDtypeStruct((dirs, 1, channels), F32),
            jax.ShapeDtypeStruct((dirs, states, channels), F32),
            jax.ShapeDtypeStruct((dirs, states, channels), F32),
        ],
        scratch_shapes=[
            pltpu.VMEM((states, LANES), F32),
            pltpu.VMEM((states, INNER, LANES), F32),
            pltpu.VMEM((states, length // INNER, LANES), F32),
            pltpu.VMEM((states, LANES), F32),
            pltpu.VMEM((states, LANES), F32),
        ],
    )(delta, rate, readout, grad)


def fourier(length):
    period = 4 * length
    odd = 2 * jnp.arange(length, dtype=jnp.int32)[:, None] + 1
    unit = 2.0 * math.pi / period

    def table(times):
        angle = ((odd * times[None, :]) % period).astype(F32) * unit
        return jnp.cos(angle), jnp.sin(angle)

    fine_cos, fine_sin = table(jnp.arange(LANES, dtype=jnp.int32))
    wide_cos, wide_sin = table(jnp.arange(length // LANES, dtype=jnp.int32) * LANES)
    cos_parts = []
    sin_parts = []
    for j in range(length // LANES):
        c, s = wide_cos[:, j : j + 1], wide_sin[:, j : j + 1]
        cos_parts.append(c * fine_cos - s * fine_sin)
        sin_parts.append(s * fine_cos + c * fine_sin)
    whole = jnp.concatenate(
        [jnp.concatenate(cos_parts, axis=1), jnp.concatenate(sin_parts, axis=1)], axis=0
    )
    return whole.astype(BF)


def make_shards(tensor_size):
    core_swap = [(i, i ^ 1) for i in range(tensor_size)]
    far_swap = [(i, i ^ 2) for i in range(tensor_size)]

    def near(v):
        return lax.ppermute(v, "tensor", core_swap)

    def far(v):
        return lax.ppermute(v, "tensor", far_swap)

    def shards(
        inputs,
        cotangent,
        lengths,
        norm_gain,
        norm_bias,
        value_weight,
        value_bias,
        feed_weight,
        feed_bias,
        mix_forward,
        mix_backward,
        mix_bias,
        out_weight,
        out_bias,
        state_delta,
        state_rate,
        state_readout,
        state_skip,
    ):
        slots, length, width = inputs.shape
        channels = feed_weight.shape[1]
        hidden_width = value_weight.shape[1]
        me = lax.axis_index("tensor")
        core = me % 2
        half = length // 2

        first_own = jnp.concatenate([feed_weight, value_weight], axis=1)
        first_all = lax.all_gather(first_own, "dp", axis=0, tiled=True)
        mix_own = jnp.concatenate([mix_forward.T, mix_backward.T], axis=1)
        mix_all = lax.all_gather(mix_own, "dp", axis=0, tiled=True)
        out_all = lax.all_gather(out_weight.T, "dp", axis=0, tiled=True)
        feed_full = first_all[:, :channels]
        value_full = first_all[:, channels:]
        mix_blocks = mix_all.reshape(tensor_size, hidden_width, 2 * channels)
        mix_of = [
            lax.dynamic_index_in_dim(mix_blocks, me ^ j, axis=0, keepdims=False)
            for j in range(tensor_size)
        ]
        mix_send = jnp.concatenate([mix_of[1], mix_of[3]], axis=0)

        delta = state_delta[:, None, :]
        rate = jnp.swapaxes(state_rate, 1, 2)
        readout = jnp.swapaxes(state_readout, 1, 2)
        wave = fourier(length)
        response = impulse(delta, rate, readout, length)
        response_f = dot_nn(wave, response.astype(BF))
        k0c, k1c = response_f[:length, :channels], response_f[:length, channels:]
        k0s, k1s = response_f[length:, :channels], response_f[length:, channels:]
        scale = 1.0 / length

        time_at = jnp.arange(length)[:, None]
        skip_row = state_skip.reshape(1, 2 * channels)

        saved = []
        layer_rows = []
        grad_mix = [None] * tensor_size
        for slot in range(slots):
            rows = inputs[slot].astype(F32)
            live = (time_at < lengths[slot]).astype(F32)
            center = rows - jnp.mean(rows, axis=-1, keepdims=True)
            spread = jnp.mean(center * center, axis=-1, keepdims=True)
            normed = (center * lax.rsqrt(spread + EPSILON) * norm_gain + norm_bias).astype(BF)
            feed_pre = dot_nn(normed, feed_full) + feed_bias
            signal = gelu_pair(feed_pre)[0] * live
            signal_low = signal.astype(BF)
            signal_f = dot_nn(wave, signal_low)
            uc, us = signal_f[:length], signal_f[length:]
            product = jnp.concatenate(
                [
                    jnp.concatenate([uc * k0c - us * k0s, uc * k1c + us * k1s], axis=1),
                    jnp.concatenate([uc * k0s + us * k0c, us * k1c - uc * k1s], axis=1),
                ],
                axis=0,
            )
            scanned = dot_tn(wave, (product * scale).astype(BF))
            both = (scanned + skip_row * jnp.concatenate([signal, signal], axis=1)).astype(BF)

            sent = dot_nt(both, mix_send).astype(BF)
            received = near(sent)
            passed = (dot_nt(both, mix_of[2]) + received[:, hidden_width:].astype(F32)).astype(BF)
            own = dot_nt(both, mix_of[0]) + received[:, :hidden_width].astype(F32)
            mixed = own + far(passed).astype(F32) + mix_bias

            value_pre = dot_nn(normed, value_full) + value_bias
            upstream_low = (cotangent[slot].astype(F32) * live).astype(BF)
            grad_hidden = dot_nn(upstream_low, out_all)
            saved.append((normed, feed_pre, live, signal, uc, us, both, mixed, value_pre, upstream_low, grad_hidden))

        grads = []
        for slot in range(slots):
            normed, feed_pre, live, signal, uc, us, both, mixed, value_pre, upstream_low, grad_hidden = saved[slot]
            value_act, value_slope = gelu_pair(value_pre)
            gate_act, gate_slope = gelu_pair(mixed)
            hidden = (gate_act * value_act).astype(BF)
            grad_gate = (gate_slope * grad_hidden * value_act).astype(BF)
            grad_value = (value_slope * grad_hidden * gate_act).astype(BF)
            pieces = [grad_gate, near(grad_gate), far(grad_gate)]
            pieces.append(near(pieces[2]))
            grads.append((hidden, grad_value, pieces))

        grad_value_w = None
        grad_out_w = None
        for slot in range(slots):
            normed, feed_pre, live, signal, uc, us, both, mixed, value_pre, upstream_low, grad_hidden = saved[slot]
            hidden, grad_value, pieces = grads[slot]
            branch = dot_nt(hidden, out_all)
            give = lax.dynamic_slice_in_dim(branch, (1 - core) * half, half, 0).astype(BF)
            keep = lax.dynamic_slice_in_dim(branch, core * half, half, 0)
            pair = lax.optimization_barrier((keep + near(give).astype(F32)).astype(BF))
            other = far(pair)
            rows_half = lax.dynamic_slice_in_dim(inputs[slot], core * half, half, 0).astype(F32)
            live_half = lax.dynamic_slice_in_dim(live, core * half, half, 0)
            mine = (
                live_half * (rows_half + (pair.astype(F32) + other.astype(F32)) + out_bias)
            ).astype(BF)
            theirs = near(mine)
            layer_rows.append(
                jnp.concatenate(
                    [jnp.where(core == 0, mine, theirs), jnp.where(core == 0, theirs, mine)], axis=0
                )
            )
            step_value = dot_tn(normed, grad_value)
            step_out = dot_tn(upstream_low, hidden)
            grad_value_w = step_value if slot == 0 else grad_value_w + step_value
            grad_out_w = step_out if slot == 0 else grad_out_w + step_out
        early = lax.psum_scatter(
            jnp.concatenate([grad_value_w.astype(BF), grad_out_w.astype(BF)], axis=1),
            "dp",
            scatter_dimension=0,
            tiled=True,
        ).astype(F32)

        input_rows = []
        grad_k = None
        grad_feed_w = None
        small = None
        for slot in range(slots):
            normed, feed_pre, live, signal, uc, us, both, mixed, value_pre, upstream_low, grad_hidden = saved[slot]
            hidden, grad_value, pieces = grads[slot]
            grad_both = dot_nn(pieces[0], mix_of[0])
            for j in (1, 2, 3):
                grad_both = grad_both + dot_nn(pieces[j], mix_of[j])
            for j in range(tensor_size):
                step = dot_tn(pieces[j], both)
                grad_mix[j] = step if slot == 0 else grad_mix[j] + step
            grad_f = dot_nn(wave, grad_both.astype(BF))
            ac, bc = grad_f[:length, :channels], grad_f[:length, channels:]
            as_, bs = grad_f[length:, :channels], grad_f[length:, channels:]
            back = jnp.concatenate(
                [
                    ac * k0c + as_ * k0s + bc * k1c - bs * k1s,
                    as_ * k0c - ac * k0s + bc * k1s + bs * k1c,
                ],
                axis=0,
            )
            grad_signal = dot_tn(wave, (back * scale).astype(BF))
            grad_signal = (
                grad_signal
                + state_skip[0] * grad_both[:, :channels]
                + state_skip[1] * grad_both[:, channels:]
            )
            lag = jnp.concatenate(
                [
                    jnp.concatenate([ac * uc + as_ * us, uc * bc + us * bs], axis=1),
                    jnp.concatenate([as_ * uc - ac * us, us * bc - uc * bs], axis=1),
                ],
                axis=0,
            )
            grad_k = lag if slot == 0 else grad_k + lag
            grad_skip = jnp.sum(grad_both * jnp.concatenate([signal, signal], axis=1), axis=0)
            grad_feed = (gelu_pair(feed_pre)[1] * live * grad_signal).astype(BF)
            features = dot_nt(grad_value, value_full) + dot_nt(grad_feed, feed_full)
            step_feed = dot_tn(normed, grad_feed)
            grad_feed_w = step_feed if slot == 0 else grad_feed_w + step_feed

            give = lax.dynamic_slice_in_dim(features, (1 - core) * half, half, 0).astype(BF)
            keep = lax.dynamic_slice_in_dim(features, core * half, half, 0)
            pair = lax.optimization_barrier((keep + near(give).astype(F32)).astype(BF))
            total = pair.astype(F32) + far(pair).astype(F32)
            rows = lax.dynamic_slice_in_dim(inputs[slot], core * half, half, 0).astype(F32)
            up_half = lax.dynamic_slice_in_dim(upstream_low, core * half, half, 0).astype(F32)
            center = rows - jnp.mean(rows, axis=-1, keepdims=True)
            spread = jnp.mean(center * center, axis=-1, keepdims=True)
            inverse = lax.rsqrt(spread + EPSILON)
            unit = center * inverse
            weighted = total * norm_gain
            mine = (
                up_half
                + (
                    weighted
                    - jnp.mean(weighted, axis=-1, keepdims=True)
                    - unit * jnp.mean(weighted * unit, axis=-1, keepdims=True)
                )
                * inverse
            ).astype(BF)
            theirs = near(mine)
            input_rows.append(
                jnp.concatenate(
                    [jnp.where(core == 0, mine, theirs), jnp.where(core == 0, theirs, mine)], axis=0
                )
            )
            now = (
                jnp.sum(total * unit, axis=0),
                jnp.sum(total, axis=0),
                jnp.sum(grad_value.astype(F32), axis=0),
                jnp.sum(grad_feed.astype(F32), axis=0),
                jnp.sum(pieces[0].astype(F32), axis=0),
                jnp.sum(upstream_low.astype(F32), axis=0),
                grad_skip,
            )
            small = now if slot == 0 else tuple(a + b for a, b in zip(small, now))

        mix_stack = jnp.stack([g.astype(BF) for g in grad_mix], axis=0)
        mix_natural = jnp.concatenate(
            [lax.dynamic_index_in_dim(mix_stack, me ^ b, axis=0, keepdims=False) for b in range(tensor_size)],
            axis=0,
        )
        mix_sum = lax.psum_scatter(mix_natural, "dp", scatter_dimension=0, tiled=True).astype(F32)
        feed_sum = lax.psum_scatter(
            grad_feed_w.astype(BF), "dp", scatter_dimension=0, tiled=True
        ).astype(F32)

        grad_response = dot_tn(wave, (grad_k * scale).astype(BF))
        grad_delta, grad_rate, grad_readout = state_grad(delta, rate, readout, grad_response)

        flat = jnp.concatenate([v.reshape(-1) for v in small] + [grad_delta.reshape(-1)])
        sums = lax.psum(flat, "dp")
        state_sums = lax.psum(jnp.concatenate([grad_rate, grad_readout], axis=0), "dp")
        at = 0
        parts = []
        for v in small + (grad_delta,):
            parts.append(sums[at : at + v.size])
            at += v.size
        norm_sums = jnp.stack([parts[0], parts[1]])
        norm_sums = norm_sums + near(norm_sums)
        state_sums = jnp.swapaxes(state_sums, 1, 2)

        return (
            jnp.stack(layer_rows),
            jnp.stack(input_rows),
            norm_sums[0],
            norm_sums[1],
            early[:, :hidden_width],
            parts[2],
            feed_sum,
            parts[3],
            mix_sum[:, :channels].T,
            mix_sum[:, channels:].T,
            parts[4],
            early[:, hidden_width:].T,
            parts[5],
            parts[7].reshape(2, channels),
            state_sums[:2],
            state_sums[2:],
            parts[6].reshape(2, channels),
        )

    return shards


def solution(mesh):
    placed = (
        P("dp", None, None),
        P("dp", None, None),
        P("dp"),
        P(),
        P(),
        P("dp", "tensor"),
        P("tensor"),
        P("dp", "tensor"),
        P("tensor"),
        P("tensor", "dp"),
        P("tensor", "dp"),
        P("tensor"),
        P("tensor", "dp"),
        P(),
        P(None, "tensor"),
        P(None, "tensor", None),
        P(None, "tensor", None),
        P(None, "tensor"),
    )
    return jax.shard_map(
        make_shards(mesh.shape["tensor"]),
        mesh=mesh,
        in_specs=placed,
        out_specs=(
            P("dp", None, None),
            P("dp", None, None),
            P(),
            P(),
            P("dp", "tensor"),
            P("tensor"),
            P("dp", "tensor"),
            P("tensor"),
            P("tensor", "dp"),
            P("tensor", "dp"),
            P("tensor"),
            P("tensor", "dp"),
            P(),
            P(None, "tensor"),
            P(None, "tensor", None),
            P(None, "tensor", None),
            P(None, "tensor"),
        ),
        check_vma=False,
    )
```

```python
import functools
import math

import jax
import jax.numpy as jnp
import numpy as np
from jax import lax
from jax.experimental import pallas as pl
from jax.experimental.pallas import tpu as pltpu
from jax.sharding import PartitionSpec as P

EPSILON = 1e-05
LANES = 128
INNER = 32
BAND = 256
ROWS = 256
BF = jnp.bfloat16
F32 = jnp.float32
GELU_C = math.sqrt(2.0 / math.pi)
GELU_A = 0.044715


def gelu_pair(x):
    square = x * x
    bend = jnp.tanh(GELU_C * x * (1.0 + GELU_A * square))
    half = 0.5 * (1.0 + bend)
    slope = half + 0.5 * x * (1.0 - bend * bend) * (GELU_C * (1.0 + 3.0 * GELU_A * square))
    return x * half, slope


def after(value, *others):
    return lax.optimization_barrier((value,) + others)[0]


def dot_nt(a, b):
    return lax.dot_general(a, b, (((1,), (1,)), ((), ())), preferred_element_type=F32)


def dot_tn(a, b):
    return lax.dot_general(a, b, (((0,), (0,)), ((), ())), preferred_element_type=F32)


def dot_nn(a, b):
    return jnp.dot(a, b, preferred_element_type=F32)


def fill_powers(rate_ref, one_ref, many_ref, scale):
    states = rate_ref.shape[0]
    offset = lax.broadcasted_iota(jnp.int32, (INNER, LANES), 0).astype(F32)

    def body(n, _):
        row = rate_ref[pl.ds(n, 1), :]
        one_ref[n] = jnp.exp(-(row * offset))
        wide = jnp.exp(-(row * (offset * float(INNER))))
        if scale is not None:
            wide = wide * scale[pl.ds(n, 1), :]
        many_ref[n] = wide
        return 0

    lax.fori_loop(0, states, body, 0)


def impulse_kernel(delta_ref, rate_ref, readout_ref, out_ref, a_ref, w_ref, one_ref, many_ref):
    states = rate_ref.shape[1]
    length = out_ref.shape[0]
    step = jnp.exp(delta_ref[0])
    a_ref[...] = step * rate_ref[0]
    w_ref[...] = step * readout_ref[0]
    fill_powers(a_ref, one_ref, many_ref, w_ref)
    group = 8
    for start in range(0, length // INNER, group):

        def body(n, sums):
            base = one_ref[n]
            return tuple(
                total + many_ref[n, start + j : start + j + 1, :] * base
                for j, total in enumerate(sums)
            )

        sums = lax.fori_loop(
            0, states, body, tuple(jnp.zeros((INNER, LANES), F32) for _ in range(group))
        )
        for j, total in enumerate(sums):
            at = (start + j) * INNER
            out_ref[at : at + INNER, :] = total.astype(out_ref.dtype)


def impulse(delta, rate, readout, length, c):
    dirs, states, channels = rate.shape
    lanes = channels // LANES
    spec = pl.BlockSpec((1, states, LANES), lambda j: (c, 0, j))
    return pl.pallas_call(
        impulse_kernel,
        name="impulse",
        grid=(lanes,),
        in_specs=[pl.BlockSpec((1, 1, LANES), lambda j: (c, 0, j)), spec, spec],
        out_specs=pl.BlockSpec((length, LANES), lambda j: (0, j)),
        out_shape=jax.ShapeDtypeStruct((length, channels), BF),
        scratch_shapes=[
            pltpu.VMEM((states, LANES), F32),
            pltpu.VMEM((states, LANES), F32),
            pltpu.VMEM((states, INNER, LANES), F32),
            pltpu.VMEM((states, length // INNER, LANES), F32),
        ],
    )(delta, rate, readout)


def state_grad_kernel(
    delta_ref, rate_ref, readout_ref, grad_ref, gdelta_ref, grate_ref, greadout_ref, a_ref, one_ref, many_ref, g_ref, m_ref
):
    states = rate_ref.shape[1]
    length = grad_ref.shape[0]
    step = jnp.exp(delta_ref[0])
    a_ref[...] = step * rate_ref[0]
    fill_powers(a_ref, one_ref, many_ref, None)
    offset = lax.broadcasted_iota(jnp.int32, (INNER, LANES), 0).astype(F32)
    group = 4
    zero = jnp.zeros((INNER, LANES), F32)

    def body(i, _):
        sums = [zero] * group
        moments = [zero] * group
        for k in range(length // INNER - 1, -1, -1):
            block = grad_ref[k * INNER : (k + 1) * INNER, :]
            for j in range(group):
                sums[j] = sums[j] + many_ref[i * group + j, k : k + 1, :] * block
                if k > 0:
                    moments[j] = moments[j] + sums[j]
        for j in range(group):
            n = i * group + j
            base = one_ref[n]
            g_ref[pl.ds(n, 1), :] = jnp.sum(base * sums[j], axis=0, keepdims=True)
            m_ref[pl.ds(n, 1), :] = jnp.sum(
                base * (offset * sums[j] + float(INNER) * moments[j]), axis=0, keepdims=True
            )
        return 0

    lax.fori_loop(0, states // group, body, 0)
    rate = rate_ref[0]
    readout = readout_ref[0]
    grad_w = g_ref[...]
    grad_a = -(step * readout) * m_ref[...]
    greadout_ref[0] = step * grad_w
    grate_ref[0] = step * grad_a
    gdelta_ref[0] = step * jnp.sum(readout * grad_w + rate * grad_a, axis=0, keepdims=True)


def state_grad(delta, rate, readout, grad, c):
    dirs, states, channels = rate.shape
    length = grad.shape[0]
    lanes = channels // LANES
    spec = pl.BlockSpec((1, states, LANES), lambda j: (c, 0, j))
    row = pl.BlockSpec((1, 1, LANES), lambda j: (c, 0, j))
    out_spec = pl.BlockSpec((1, states, LANES), lambda j: (0, 0, j))
    out_row = pl.BlockSpec((1, 1, LANES), lambda j: (0, 0, j))
    return pl.pallas_call(
        state_grad_kernel,
        name="state_grad",
        grid=(lanes,),
        in_specs=[row, spec, spec, pl.BlockSpec((length, LANES), lambda j: (0, c * lanes + j))],
        out_specs=[out_row, out_spec, out_spec],
        out_shape=[
            jax.ShapeDtypeStruct((1, 1, channels), F32),
            jax.ShapeDtypeStruct((1, states, channels), F32),
            jax.ShapeDtypeStruct((1, states, channels), F32),
        ],
        scratch_shapes=[
            pltpu.VMEM((states, LANES), F32),
            pltpu.VMEM((states, INNER, LANES), F32),
            pltpu.VMEM((states, length // INNER, LANES), F32),
            pltpu.VMEM((states, LANES), F32),
            pltpu.VMEM((states, LANES), F32),
        ],
    )(delta, rate, readout, grad)


def whole(shape):
    return pl.BlockSpec(shape, lambda *at: (0,) * len(shape), pipeline_mode=pl.Buffered(1))


def out(shape):
    return pl.BlockSpec(shape, lambda *at: (0,) * len(shape))


def by_rows(width):
    return pl.BlockSpec((ROWS, width), lambda i, *at: (i, 0))


def response_kernel(first_ref, second_ref, rows_ref, turn_ref, k_ref):
    channels = first_ref.shape[1]
    length = first_ref.shape[0]
    tile = lambda v: jnp.concatenate([v] * (channels // LANES), axis=1)
    c, s = tile(turn_ref[0]), tile(turn_ref[1])
    for i, ref in enumerate((first_ref, second_ref)):
        f = dot_nn(rows_ref[...], ref[...]) * (1.0 / length)
        p, q = f[:BAND], f[BAND:]
        at = slice(i * channels, (i + 1) * channels)
        k_ref[0, 0, :, at] = c * p + s * q
        k_ref[0, 1, :, at] = c * q - s * p


def response(first, second, rows, turn):
    length, channels = first.shape
    bands = length // BAND
    return pl.pallas_call(
        response_kernel,
        name="response",
        grid=(bands,),
        in_specs=[
            whole((length, channels)),
            whole((length, channels)),
            pl.BlockSpec((2 * BAND, length), lambda b: (b, 0)),
            pl.BlockSpec((2, BAND, LANES), lambda b: (0, b, 0)),
        ],
        out_specs=pl.BlockSpec((1, 2, BAND, 2 * channels), lambda b: (b, 0, 0, 0)),
        out_shape=jax.ShapeDtypeStruct((bands, 2, BAND, 2 * channels), F32),
        compiler_params=pltpu.CompilerParams(vmem_limit_bytes=56 << 20),
    )(first, second, rows, turn)


def response_grad_kernel(lag_ref, cols_ref, turn_ref, out_ref):
    length, channels = out_ref.shape
    tile = lambda v: jnp.concatenate([v] * (channels // LANES), axis=1)
    c, s = tile(turn_ref[0]) * (1.0 / length), tile(turn_ref[1]) * (1.0 / length)
    p, q = lag_ref[:BAND], lag_ref[BAND:]
    turned = jnp.concatenate([(c * p - s * q).astype(BF), (s * p + c * q).astype(BF)], axis=0)
    step = dot_nn(cols_ref[...], turned)

    @pl.when(pl.program_id(0) == 0)
    def _():
        out_ref[...] = step

    @pl.when(pl.program_id(0) > 0)
    def _():
        out_ref[...] += step


def response_grad(lag, cols, turn):
    length = cols.shape[0]
    channels = lag.shape[1]
    return pl.pallas_call(
        response_grad_kernel,
        name="response_grad",
        grid=(length // BAND,),
        in_specs=[
            pl.BlockSpec((2 * BAND, channels), lambda b: (b, 0)),
            pl.BlockSpec((length, 2 * BAND), lambda b: (0, b)),
            pl.BlockSpec((2, BAND, LANES), lambda b: (0, b, 0)),
        ],
        out_specs=out((length, channels)),
        out_shape=jax.ShapeDtypeStruct((length, channels), F32),
        compiler_params=pltpu.CompilerParams(vmem_limit_bytes=56 << 20),
    )(lag, cols, turn)


def send_kernel(a_ref, first_ref, second_ref, first_out, second_out):
    first_out[...] = dot_nn(a_ref[...], first_ref[...]).astype(BF)
    second_out[...] = dot_nn(a_ref[...], second_ref[...]).astype(BF)


def send(a, first, second):
    length, width = a.shape
    n = first.shape[1]
    return pl.pallas_call(
        send_kernel,
        name="send",
        grid=(length // ROWS,),
        in_specs=[by_rows(width), whole((width, n)), whole((width, n))],
        out_specs=[by_rows(n), by_rows(n)],
        out_shape=[jax.ShapeDtypeStruct((length, n), BF)] * 2,
    )(a, first, second)


def join_kernel(a_ref, b_ref, add_ref, out_ref):
    out_ref[...] = (dot_nn(a_ref[...], b_ref[...]) + add_ref[...].astype(F32)).astype(BF)


def join(a, b, add):
    length, width = a.shape
    n = b.shape[1]
    return pl.pallas_call(
        join_kernel,
        name="join",
        grid=(length // ROWS,),
        in_specs=[by_rows(width), whole((width, n)), by_rows(n)],
        out_specs=by_rows(n),
        out_shape=jax.ShapeDtypeStruct((length, n), BF),
    )(a, b, add)


def before_gate_kernel(
    slot, length_ref, both_ref, mix_ref, near_ref, mix_bias_ref, normed_ref, value_ref, value_bias_ref,
    cot_ref, out_ref, part_ref, act_ref, first_ref, second_ref, up_ref, sum_ref,
):
    i = pl.program_id(0)
    part_ref[...] = dot_nn(both_ref[...], mix_ref[...]) + near_ref[...].astype(F32) + mix_bias_ref[...]
    act, slope = gelu_pair(dot_nn(normed_ref[...], value_ref[...]) + value_bias_ref[...])
    cot = cot_ref[0].astype(F32)
    time_at = lax.broadcasted_iota(jnp.int32, cot.shape, 0) + i * ROWS
    upstream = jnp.where(time_at < length_ref[slot], cot, 0.0)
    low = upstream.astype(BF)
    grad_hidden = dot_nn(low, out_ref[...])
    act_ref[...] = act
    first_ref[...] = grad_hidden * act
    second_ref[...] = grad_hidden * slope
    up_ref[...] = low

    @pl.when(i == 0)
    def _():
        sum_ref[...] = jnp.zeros_like(sum_ref)

    sum_ref[...] += jnp.sum(upstream, axis=0, keepdims=True)


def before_gate(both, mix, near, mix_bias, normed, last_all, value_bias, cotangent, lengths, slot):
    length, width = normed.shape
    n = mix.shape[1]
    return pl.pallas_call(
        functools.partial(before_gate_kernel, slot),
        name="before_gate",
        grid_spec=pltpu.PrefetchScalarGridSpec(
            num_scalar_prefetch=1,
            grid=(length // ROWS,),
            in_specs=[
                by_rows(both.shape[1]),
                whole(mix.shape),
                by_rows(n),
                whole((1, n)),
                by_rows(width),
                whole((width, n)),
                whole((1, n)),
                pl.BlockSpec((1, ROWS, width), lambda i, *at: (slot, i, 0)),
                pl.BlockSpec((width, n), lambda *at: (0, 1), pipeline_mode=pl.Buffered(1)),
            ],
            out_specs=[by_rows(n)] * 4 + [by_rows(width), out((1, width))],
        ),
        out_shape=[jax.ShapeDtypeStruct((length, n), F32)] * 4
        + [jax.ShapeDtypeStruct((length, width), BF), jax.ShapeDtypeStruct((1, width), F32)],
        compiler_params=pltpu.CompilerParams(vmem_limit_bytes=56 << 20),
    )(lengths, both, mix, near, mix_bias, normed, last_all, value_bias, cotangent, last_all)


def gate_kernel(part_ref, far_ref, act_ref, first_ref, second_ref, hidden_ref, gate_ref, value_ref, sum_ref):
    gate_act, gate_slope = gelu_pair(part_ref[...] + far_ref[...].astype(F32))
    hidden_ref[...] = (gate_act * act_ref[...]).astype(BF)
    gate = (gate_slope * first_ref[...]).astype(BF)
    value = (gate_act * second_ref[...]).astype(BF)
    gate_ref[...] = gate
    value_ref[...] = value

    @pl.when(pl.program_id(0) == 0)
    def _():
        sum_ref[...] = jnp.zeros_like(sum_ref)

    sum_ref[0:1, :] += jnp.sum(gate.astype(F32), axis=0, keepdims=True)
    sum_ref[1:2, :] += jnp.sum(value.astype(F32), axis=0, keepdims=True)


def gate(part, far, act, first, second):
    length, n = part.shape
    return pl.pallas_call(
        gate_kernel,
        name="gate",
        grid=(length // ROWS,),
        in_specs=[by_rows(n)] * 5,
        out_specs=[by_rows(n)] * 3 + [out((2, n))],
        out_shape=[jax.ShapeDtypeStruct((length, n), BF)] * 3 + [jax.ShapeDtypeStruct((2, n), F32)],
        compiler_params=pltpu.CompilerParams(vmem_limit_bytes=56 << 20),
    )(part, far, act, first, second)


def tables(length):
    odd = 2 * np.arange(length, dtype=np.int64) + 1
    angle = (odd[:, None] * odd[None, :]) % (8 * length) * (math.pi / (4 * length))
    bands = length // BAND
    both = np.stack([np.cos(angle).reshape(bands, BAND, length), np.sin(angle).reshape(bands, BAND, length)], axis=1)
    rows = both.reshape(2 * length, length)
    turn = odd * (math.pi / (4 * length))
    return rows.astype(BF), np.ascontiguousarray(rows.T).astype(BF), np.repeat(
        np.stack([np.cos(turn), np.sin(turn)])[:, :, None], LANES, axis=2
    ).astype(np.float32)

def conv_forward_kernel(slot, length_ref, normed_ref, weight_ref, bias_ref, rows_ref, cols_ref, k_ref, skip_ref, slope_ref, low_ref, u_ref, both_ref, total_ref):
    band = pl.program_id(0)
    length, channels = slope_ref.shape

    @pl.when(band == 0)
    def _():
        def body(i, _):
            at = pl.ds(pl.multiple_of(i * 256, 256), 256)
            pre = dot_nn(normed_ref[at, :], weight_ref[...]) + bias_ref[...]
            value, slope = gelu_pair(pre)
            time_at = lax.broadcasted_iota(jnp.int32, pre.shape, 0) + i * 256
            live = jnp.where(time_at < length_ref[slot], 1.0, 0.0)
            signal = value * live
            slope_ref[at, :] = slope * live
            low_ref[at, :] = signal.astype(BF)
            total_ref[at, :channels] = skip_ref[0:1, :] * signal
            total_ref[at, channels:] = skip_ref[1:2, :] * signal
            return 0
        lax.fori_loop(0, length // 256, body, 0)

    u = dot_nn(rows_ref[...], low_ref[...])
    u_ref[...] = u
    uc, us = u[:BAND], u[BAND:]
    k0c, k1c = k_ref[0, 0, :, :channels], k_ref[0, 0, :, channels:]
    k0s, k1s = k_ref[0, 1, :, :channels], k_ref[0, 1, :, channels:]
    product = jnp.concatenate(
        [
            jnp.concatenate([uc * k0c - us * k0s, uc * k1c + us * k1s], axis=1).astype(BF),
            jnp.concatenate([uc * k0s + us * k0c, us * k1c - uc * k1s], axis=1).astype(BF),
        ],
        axis=0,
    )
    total_ref[...] += dot_nn(cols_ref[...], product)

    @pl.when(band == pl.num_programs(0) - 1)
    def _():
        both_ref[...] = total_ref[...].astype(BF)

def conv_forward(normed, weight, bias, k, skip, lengths, rows, cols, slot):
    length, width = normed.shape
    channels = weight.shape[1]
    bands = length // BAND
    return pl.pallas_call(
        functools.partial(conv_forward_kernel, slot),
        name="conv_forward",
        grid_spec=pltpu.PrefetchScalarGridSpec(
            num_scalar_prefetch=1,
            grid=(bands,),
            in_specs=[
                whole((length, width)), whole((width, channels)), whole((1, channels)),
                pl.BlockSpec((2 * BAND, length), lambda b, n: (b, 0)),
                pl.BlockSpec((length, 2 * BAND), lambda b, n: (0, b)),
                pl.BlockSpec((1, 2, BAND, 2 * channels), lambda b, n: (b, 0, 0, 0)),
                whole((2, channels)),
            ],
            out_specs=[
                out((length, channels)), out((length, channels)),
                pl.BlockSpec((2 * BAND, channels), lambda b, n: (b, 0)),
                out((length, 2 * channels)),
            ],
            scratch_shapes=[pltpu.VMEM((length, 2 * channels), F32)],
        ),
        out_shape=[
            jax.ShapeDtypeStruct((length, channels), F32),
            jax.ShapeDtypeStruct((length, channels), BF),
            jax.ShapeDtypeStruct((2 * length, channels), F32),
            jax.ShapeDtypeStruct((length, 2 * channels), BF),
        ],
        compiler_params=pltpu.CompilerParams(vmem_limit_bytes=56 << 20),
    )(lengths, normed, weight, bias, rows, cols, k, skip)

def conv_backward_kernel(count, *refs):
    pieces, mixes = refs[:count], refs[count:2 * count]
    rows_ref, cols_ref, k_ref, u_ref, slope_ref, low_ref, skip_ref, before_ref, feed_ref, lag_ref, skips_ref, both_ref, total_ref = refs[2 * count:]
    band = pl.program_id(0)
    length, channels = slope_ref.shape

    @pl.when(band == 0)
    def _():
        def body(i, sums):
            at = pl.ds(pl.multiple_of(i * 256, 256), 256)
            both = dot_nt(pieces[0][at, :], mixes[0][...])
            for piece, mix in zip(pieces[1:], mixes[1:]):
                both = both + dot_nt(piece[at, :], mix[...])
            both_ref[at, :] = both.astype(BF)
            total_ref[at, :] = skip_ref[0:1, :] * both[:, :channels] + skip_ref[1:2, :] * both[:, channels:]
            signal = low_ref[at, :].astype(F32)
            return sums + jnp.sum(both * jnp.concatenate([signal, signal], axis=1), axis=0, keepdims=True)
        skips_ref[...] = lax.fori_loop(0, length // 256, body, jnp.zeros((1, 2 * channels), F32))

    g = dot_nn(rows_ref[...], both_ref[...])
    ac, bc = g[:BAND, :channels], g[:BAND, channels:]
    as_, bs = g[BAND:, :channels], g[BAND:, channels:]
    uc, us = u_ref[:BAND], u_ref[BAND:]
    k0c, k1c = k_ref[0, 0, :, :channels], k_ref[0, 0, :, channels:]
    k0s, k1s = k_ref[0, 1, :, :channels], k_ref[0, 1, :, channels:]
    back = jnp.concatenate(
        [
            (ac * k0c + as_ * k0s + bc * k1c - bs * k1s).astype(BF),
            (as_ * k0c - ac * k0s + bc * k1s + bs * k1c).astype(BF),
        ],
        axis=0,
    )
    if before_ref is None:
        lag_ref[:BAND, :channels] = ac * uc + as_ * us
        lag_ref[:BAND, channels:] = uc * bc + us * bs
        lag_ref[BAND:, :channels] = as_ * uc - ac * us
        lag_ref[BAND:, channels:] = us * bc - uc * bs
    else:
        lag_ref[:BAND, :channels] = before_ref[:BAND, :channels] + ac * uc + as_ * us
        lag_ref[:BAND, channels:] = before_ref[:BAND, channels:] + uc * bc + us * bs
        lag_ref[BAND:, :channels] = before_ref[BAND:, :channels] + as_ * uc - ac * us
        lag_ref[BAND:, channels:] = before_ref[BAND:, channels:] + us * bc - uc * bs
    total_ref[...] += dot_nn(cols_ref[...], back)

    @pl.when(band == pl.num_programs(0) - 1)
    def _():
        feed_ref[...] = (slope_ref[...] * total_ref[...]).astype(BF)

def conv_backward(pieces, mixes, k, u, slope, low, skip, rows, cols, before):
    length, channels = slope.shape
    width = pieces[0].shape[1]
    bands = length // BAND
    band_spec = pl.BlockSpec((2 * BAND, 2 * channels), lambda b: (b, 0))
    count = len(pieces)
    def kernel(*refs):
        at = 2 * count + 7
        if before is None: refs = refs[:at] + (None,) + refs[at:]
        conv_backward_kernel(count, *refs)
    return pl.pallas_call(
        kernel,
        name="conv_backward",
        grid=(bands,),
        in_specs=[whole((length, width))] * count + [whole((2 * channels, width))] * count + [
            pl.BlockSpec((2 * BAND, length), lambda b: (b, 0)),
            pl.BlockSpec((length, 2 * BAND), lambda b: (0, b)),
            pl.BlockSpec((1, 2, BAND, 2 * channels), lambda b: (b, 0, 0, 0)),
            pl.BlockSpec((2 * BAND, channels), lambda b: (b, 0)),
            whole((length, channels)), whole((length, channels)), whole((2, channels)),
        ] + ([] if before is None else [band_spec]),
        out_specs=[out((length, channels)), band_spec, out((1, 2 * channels))],
        out_shape=[
            jax.ShapeDtypeStruct((length, channels), BF),
            jax.ShapeDtypeStruct((2 * length, 2 * channels), F32),
            jax.ShapeDtypeStruct((1, 2 * channels), F32),
        ],
        scratch_shapes=[pltpu.VMEM((length, 2 * channels), BF), pltpu.VMEM((length, channels), F32)],
        compiler_params=pltpu.CompilerParams(vmem_limit_bytes=60 << 20),
    )(*pieces, *mixes, rows, cols, k, u, slope, low, skip, *(() if before is None else (before,)))


def make_shards(dp_size, tensor_size):
    core_swap = [(i, i ^ 1) for i in range(tensor_size)]
    far_swap = [(i, i ^ 2) for i in range(tensor_size)]
    parts_of = dp_size // tensor_size

    def near(v):
        return lax.ppermute(v, "tensor", core_swap)

    def far(v):
        return lax.ppermute(v, "tensor", far_swap)

    def across(v, mask):
        return lax.ppermute(v, "dp", [(i, i ^ mask) for i in range(dp_size)])

    def shards(
        inputs,
        cotangent,
        lengths,
        norm_gain,
        norm_bias,
        value_weight,
        value_bias,
        feed_weight,
        feed_bias,
        mix_forward,
        mix_backward,
        mix_bias,
        out_weight,
        out_bias,
        state_delta,
        state_rate,
        state_readout,
        state_skip,
    ):
        slots, length, width = inputs.shape
        channels = feed_weight.shape[1]
        hidden_width = value_weight.shape[1]
        states = state_rate.shape[2]
        me = lax.axis_index("tensor")
        rank = lax.axis_index("dp")
        core = me % 2
        half = length // 2

        def collect(v):
            whole_v = v[None]
            mask = dp_size // 2
            stages = []
            while mask:
                stages.append(whole_v)
                other = across(whole_v, mask)
                upper = (rank & mask) != 0
                whole_v = jnp.stack(
                    [jnp.where(upper, other, whole_v), jnp.where(upper, whole_v, other)], axis=1
                )
                whole_v = whole_v.reshape((-1,) + v.shape)
                mask //= 2
            return whole_v.reshape((-1,) + v.shape[1:]), stages

        class Halving:
            def __init__(self, blocks):
                self.blocks = blocks
                self.give = None

            def launch(self, mask, flip=False):
                upper = ((rank & mask) != 0) ^ flip
                pairs = list(zip(self.blocks[::2], self.blocks[1::2]))
                self.give = jnp.concatenate(
                    [jnp.where(upper, a, b).astype(BF) for a, b in pairs], axis=0
                )
                self.blocks = [jnp.where(upper, b, a) for a, b in pairs]
                self.got = across(self.give, mask)
                return self

            def land(self, *anchors):
                got = after(self.got, *anchors)
                size = self.blocks[0].shape[0]
                self.blocks = [
                    b + got[i * size : (i + 1) * size].astype(F32) for i, b in enumerate(self.blocks)
                ]
                return self

        def row_blocks(v):
            size = v.shape[0] // dp_size
            return [v[i * size : (i + 1) * size] for i in range(dp_size)]

        def total_over_dp(v):
            mask = 1
            while mask < dp_size:
                v = v + across(v, mask)
                mask *= 2
            return v

        feed_full, feed_stages = collect(feed_weight)
        mix_own = jnp.concatenate([mix_forward, mix_backward], axis=0)
        mix_all = lax.all_gather(mix_own, "dp", axis=0, tiled=False)
        last_own = jnp.concatenate([value_weight, out_weight.T], axis=1)
        last_all = lax.all_gather(last_own, "dp", axis=0, tiled=True)
        mix_groups = mix_all.reshape((tensor_size, parts_of) + mix_own.shape)
        mix_of = []
        for j in range(tensor_size):
            quarter = lax.dynamic_index_in_dim(mix_groups, me ^ j, axis=0, keepdims=False)
            mix_of.append(jnp.concatenate([quarter[i] for i in range(parts_of)], axis=1))

        delta = state_delta[:, None, :]
        rate = jnp.swapaxes(state_rate, 1, 2)
        readout = jnp.swapaxes(state_readout, 1, 2)
        fourier_rows, fourier_cols, turn = (jnp.asarray(v) for v in tables(length))
        pulses = [
            impulse(after(delta, feed_stages[c - 2]), rate, readout, length, c) for c in range(2)
        ]
        spectra = response(pulses[0], pulses[1], fourier_rows, turn)

        time_at = jnp.arange(length)[:, None]
        normed, slope, low, u, both = [], [], [], [], []
        for slot in range(slots):
            rows = inputs[slot].astype(F32)
            center = rows - jnp.mean(rows, axis=-1, keepdims=True)
            spread = jnp.mean(center * center, axis=-1, keepdims=True)
            normed.append((center * lax.rsqrt(spread + EPSILON) * norm_gain + norm_bias).astype(BF))
        for slot in range(slots):
            parts = conv_forward(
                normed[slot],
                feed_full,
                feed_bias[None, :],
                spectra,
                state_skip,
                lengths,
                fourier_rows,
                fourier_cols,
                slot,
            )
            for whole_list, part in zip((slope, low, u, both), parts):
                whole_list.append(part)

        passed = None
        near_own, passes = [], []
        for slot in range(slots):
            left = both[slot] if passed is None else after(both[slot], passed)
            to_own, to_pass = send(left, mix_of[1], mix_of[3])
            passed = join(left, mix_of[2], near(to_pass))
            near_own.append(near(to_own))
            passes.append(passed)
        last_all = after(last_all, passed)
        pre = []
        for slot in range(slots):
            pre.append(
                before_gate(
                    both[slot],
                    mix_of[0],
                    near_own[slot],
                    mix_bias[None, :],
                    normed[slot],
                    last_all,
                    value_bias[None, :],
                    cotangent,
                    lengths,
                    slot,
                )
            )
        upstream_low = [p[4] for p in pre]
        value_full = last_all[:, :hidden_width]
        out_all = last_all[:, hidden_width:]

        hidden, grad_gate, grad_value, gate_sums = [], [], [], []
        for slot in range(slots):
            arrived = far(passes[slot])
            if slot == 0:
                arrived = after(arrived, pre[-1][0])
            else:
                arrived = after(arrived, grad_gate[-1])
            parts = gate(pre[slot][0], arrived, *pre[slot][1:4])
            for whole_list, part in zip((hidden, grad_gate, grad_value, gate_sums), parts):
                whole_list.append(part)
        far_gate = [far(g) for g in grad_gate]
        near_gate = [near(g) for g in grad_gate]

        last_grad = sum(
            jnp.concatenate(
                [dot_tn(normed[slot], grad_value[slot]), dot_tn(upstream_low[slot], hidden[slot])],
                axis=1,
            )
            for slot in range(slots)
        )
        last_sum = Halving(row_blocks(last_grad)).launch(1)

        first = core == 0
        branches = [dot_nt(hidden[slot], out_all) for slot in range(slots)]
        branch_keep = jnp.where(first, branches[0], branches[1])
        branch_give = jnp.where(first, branches[1], branches[0]).astype(BF)

        def mix_blocks(pieces):
            size = hidden_width // parts_of
            blocks = []
            for quarter in pieces:
                g = sum(dot_tn(both[slot], after(quarter[slot], last_sum.give)) for slot in range(slots))
                blocks += [g[:, i * size : (i + 1) * size] for i in range(parts_of)]
            return blocks

        low_masks = [1 << i for i in range(parts_of.bit_length() - 1)]

        def finish_low(halving, *anchors):
            for mask in low_masks[1:]:
                halving.land(*anchors).launch(mask)
            return halving.land(*anchors).launch(parts_of, core == 1)

        def start_low(blocks):
            halving = Halving(blocks)
            return halving.launch(low_masks[0]) if low_masks else halving

        near_sum = start_low(mix_blocks([grad_gate, near_gate]))
        branch_pair = (branch_keep + near(branch_give).astype(F32)).astype(BF)

        early = jnp.concatenate(
            [sum(g[0:1] for g in gate_sums), sum(g[1:2] for g in gate_sums), sum(p[5] for p in pre)], axis=0
        )
        early = total_over_dp(early)

        def back(slot, arrived, lag, *anchors):
            pieces = [grad_gate[slot], near_gate[slot], arrived, near(arrived)]
            pieces[0] = after(pieces[0], *anchors)
            return pieces[3], conv_backward(
                pieces,
                mix_of,
                spectra,
                u[slot],
                slope[slot],
                low[slot],
                state_skip,
                fourier_rows,
                fourier_cols,
                lag,
            )

        def features(slot, grad_feed):
            v = dot_nt(grad_value[slot], value_full) + dot_nt(grad_feed, feed_full)
            give = lax.dynamic_slice_in_dim(v, (1 - core) * half, half, 0).astype(BF)
            keep = lax.dynamic_slice_in_dim(v, core * half, half, 0)
            return give, keep

        far_near_a, (grad_feed_a, lag, skips_a) = back(
            0, far_gate[0], None, near_sum.give, last_sum.give, branch_pair
        )
        give_a, keep_a = features(0, grad_feed_a)
        near_a = near(give_a)
        last_sum.land(grad_feed_a).launch(2)
        near_sum = finish_low(near_sum, grad_feed_a)

        arrived_b = after(far_gate[1], last_sum.give, near_sum.give, give_a)
        far_near_b = near(arrived_b)
        far_sum = start_low(mix_blocks([[far_gate[0], arrived_b], [far_near_a, far_near_b]]))
        pair_a = (keep_a + near_a.astype(F32)).astype(BF)
        far_near_b, (grad_feed_b, lag, skips_b) = back(1, arrived_b, lag, far_sum.give, pair_a)
        far_a = far(pair_a)
        last_sum.land(grad_feed_b)
        mask = 4
        while mask < dp_size:
            last_sum.launch(mask)
            mask *= 2
            if mask < dp_size:
                last_sum.land(grad_feed_b)
        give_b, keep_b = features(1, grad_feed_b)
        near_b = near(give_b)
        near_sum.land(grad_feed_b)
        far_sum = finish_low(far_sum, give_b)

        feed_sum = Halving(
            row_blocks(dot_tn(normed[0], grad_feed_a) + dot_tn(normed[1], grad_feed_b))
        ).launch(1)
        grad_response = response_grad(after(lag, give_b, far_sum.give), fourier_cols, turn)
        pair_b = (keep_b + after(near_b, grad_response).astype(F32)).astype(BF)
        far_b = far(pair_b)
        far_sum.land(grad_response)
        mix_sum = Halving([near_sum.blocks[0], far_sum.blocks[0]]).launch(2 * parts_of, me >= 2)

        def state_sums(c, *anchors):
            grad_delta, grad_rate, grad_readout = state_grad(
                delta, rate, readout, after(grad_response, *anchors), c
            )
            at = slice(c * channels, (c + 1) * channels)
            grad_skip = skips_a[:, at] + skips_b[:, at]
            return jnp.concatenate([grad_rate[0], grad_readout[0], grad_delta[0], grad_skip], axis=0)

        state_a = state_sums(0, pair_b, mix_sum.give, feed_sum.give)
        mask = 2
        feed_sum.land(state_a)
        while mask < dp_size:
            feed_sum.launch(mask)
            mask *= 2
            if mask < dp_size:
                feed_sum.land()
        state_b = state_sums(1, state_a, feed_sum.give)

        rows = jnp.where(first, inputs[0], inputs[1]).astype(F32)
        live = (time_at < jnp.where(first, lengths[0], lengths[1])).astype(F32)
        branch_far = after(far(branch_pair), pair_b)
        mine = (live * (rows + (branch_pair.astype(F32) + branch_far.astype(F32)) + out_bias)).astype(BF)
        theirs = near(mine)
        layer_out = jnp.stack([jnp.where(first, mine, theirs), jnp.where(first, theirs, mine)])

        input_rows = []
        small = None
        for slot, pair, arrived in ((0, pair_a, after(far_a, state_a)), (1, pair_b, after(far_b, state_b))):
            total = pair.astype(F32) + arrived.astype(F32)
            rows = lax.dynamic_slice_in_dim(inputs[slot], core * half, half, 0).astype(F32)
            up_half = lax.dynamic_slice_in_dim(upstream_low[slot], core * half, half, 0).astype(F32)
            center = rows - jnp.mean(rows, axis=-1, keepdims=True)
            spread = jnp.mean(center * center, axis=-1, keepdims=True)
            inverse = lax.rsqrt(spread + EPSILON)
            unit = center * inverse
            weighted = total * norm_gain
            mine = (
                up_half
                + (
                    weighted
                    - jnp.mean(weighted, axis=-1, keepdims=True)
                    - unit * jnp.mean(weighted * unit, axis=-1, keepdims=True)
                )
                * inverse
            ).astype(BF)
            theirs = near(mine)
            input_rows.append(
                jnp.concatenate(
                    [jnp.where(core == 0, mine, theirs), jnp.where(core == 0, theirs, mine)], axis=0
                )
            )
            now = jnp.concatenate(
                [jnp.sum(total * unit, axis=0, keepdims=True), jnp.sum(total, axis=0, keepdims=True)], axis=0
            )
            small = now if slot == 0 else small + now

        feed_bias_sum = jnp.sum(grad_feed_a.astype(F32), axis=0, keepdims=True) + jnp.sum(
            grad_feed_b.astype(F32), axis=0, keepdims=True
        )
        last_sum = last_sum.land(state_a).blocks[0]
        feed_sum = feed_sum.land(state_b).blocks[0]
        mix_sum = mix_sum.land(state_b).blocks[0]
        totals = [total_over_dp(state_a), total_over_dp(state_b)]
        feed_bias_sum = total_over_dp(feed_bias_sum)
        small = total_over_dp(small)
        norm_sums = small + near(small)
        last_rows = jnp.stack([v[2 * states :] for v in totals])

        return (
            layer_out,
            jnp.stack(input_rows),
            norm_sums[0],
            norm_sums[1],
            last_sum[:, :hidden_width],
            early[1],
            feed_sum,
            feed_bias_sum[0],
            mix_sum[:channels],
            mix_sum[channels:],
            early[0],
            last_sum[:, hidden_width:].T,
            early[2],
            last_rows[:, 0],
            jnp.swapaxes(jnp.stack([v[:states] for v in totals]), 1, 2),
            jnp.swapaxes(jnp.stack([v[states : 2 * states] for v in totals]), 1, 2),
            last_rows[:, 1],
        )

    return shards


def solution(mesh):
    placed = (
        P("dp", None, None),
        P("dp", None, None),
        P("dp"),
        P(),
        P(),
        P("dp", "tensor"),
        P("tensor"),
        P("dp", "tensor"),
        P("tensor"),
        P("tensor", "dp"),
        P("tensor", "dp"),
        P("tensor"),
        P("tensor", "dp"),
        P(),
        P(None, "tensor"),
        P(None, "tensor", None),
        P(None, "tensor", None),
        P(None, "tensor"),
    )
    return jax.shard_map(
        make_shards(mesh.shape["dp"], mesh.shape["tensor"]),
        mesh=mesh,
        in_specs=placed,
        out_specs=(
            P("dp", None, None),
            P("dp", None, None),
            P(),
            P(),
            P("dp", "tensor"),
            P("tensor"),
            P("dp", "tensor"),
            P("tensor"),
            P("tensor", "dp"),
            P("tensor", "dp"),
            P("tensor"),
            P("tensor", "dp"),
            P(),
            P(None, "tensor"),
            P(None, "tensor", None),
            P(None, "tensor", None),
            P(None, "tensor"),
        ),
        check_vma=False,
    )
```

```python
import functools
import math

import jax
import jax.numpy as jnp
import numpy as np
from jax import lax
from jax.experimental import pallas as pl
from jax.experimental.pallas import tpu as pltpu
from jax.sharding import PartitionSpec as P

EPSILON = 1e-05
LANES = 128
INNER = 32
BAND = 256
ROWS = 256
BF = jnp.bfloat16
F32 = jnp.float32
GELU_C = math.sqrt(2.0 / math.pi)
GELU_A = 0.044715


def gelu_pair(x):
    square = x * x
    bend = jnp.tanh(GELU_C * x * (1.0 + GELU_A * square))
    half = 0.5 * (1.0 + bend)
    slope = half + 0.5 * x * (1.0 - bend * bend) * (GELU_C * (1.0 + 3.0 * GELU_A * square))
    return x * half, slope


def after(value, *others):
    return lax.optimization_barrier((value,) + others)[0]


def dot_nt(a, b):
    return lax.dot_general(a, b, (((1,), (1,)), ((), ())), preferred_element_type=F32)


def dot_tn(a, b):
    return lax.dot_general(a, b, (((0,), (0,)), ((), ())), preferred_element_type=F32)


def dot_nn(a, b):
    return jnp.dot(a, b, preferred_element_type=F32)


def fill_powers(rate_ref, one_ref, many_ref, scale):
    states = rate_ref.shape[0]
    offset = lax.broadcasted_iota(jnp.int32, (INNER, LANES), 0).astype(F32)

    def body(n, _):
        row = rate_ref[pl.ds(n, 1), :]
        one_ref[n] = jnp.exp(-(row * offset))
        wide = jnp.exp(-(row * (offset * float(INNER))))
        if scale is not None:
            wide = wide * scale[pl.ds(n, 1), :]
        many_ref[n] = wide
        return 0

    lax.fori_loop(0, states, body, 0, unroll=8)


def impulse_kernel(delta_ref, rate_ref, readout_ref, out_ref, a_ref, w_ref, one_ref, many_ref):
    states = rate_ref.shape[1]
    length = out_ref.shape[0]
    step = jnp.exp(delta_ref[0])
    a_ref[...] = step * rate_ref[0]
    w_ref[...] = step * readout_ref[0]
    fill_powers(a_ref, one_ref, many_ref, w_ref)
    group = 8
    for start in range(0, length // INNER, group):

        def body(n, sums):
            base = one_ref[n]
            return tuple(
                total + many_ref[n, start + j : start + j + 1, :] * base
                for j, total in enumerate(sums)
            )

        sums = lax.fori_loop(
            0, states, body, tuple(jnp.zeros((INNER, LANES), F32) for _ in range(group)), unroll=8
        )
        for j, total in enumerate(sums):
            at = (start + j) * INNER
            out_ref[at : at + INNER, :] = total.astype(out_ref.dtype)


def impulse(delta, rate, readout, length, c):
    dirs, states, channels = rate.shape
    lanes = channels // LANES
    spec = pl.BlockSpec((1, states, LANES), lambda j: (c, 0, j))
    return pl.pallas_call(
        impulse_kernel,
        name="impulse",
        grid=(lanes,),
        in_specs=[pl.BlockSpec((1, 1, LANES), lambda j: (c, 0, j)), spec, spec],
        out_specs=pl.BlockSpec((length, LANES), lambda j: (0, j)),
        out_shape=jax.ShapeDtypeStruct((length, channels), BF),
        scratch_shapes=[
            pltpu.VMEM((states, LANES), F32),
            pltpu.VMEM((states, LANES), F32),
            pltpu.VMEM((states, INNER, LANES), F32),
            pltpu.VMEM((states, length // INNER, LANES), F32),
        ],
    )(delta, rate, readout)


def state_grad_kernel(
    delta_ref, rate_ref, readout_ref, grad_ref, extra_ref, out_ref, a_ref, one_ref, many_ref, g_ref, m_ref
):
    states = rate_ref.shape[1]
    length = grad_ref.shape[0]
    step = jnp.exp(delta_ref[0])
    a_ref[...] = step * rate_ref[0]
    fill_powers(a_ref, one_ref, many_ref, None)
    offset = lax.broadcasted_iota(jnp.int32, (INNER, LANES), 0).astype(F32)
    group = 4
    zero = jnp.zeros((INNER, LANES), F32)

    def body(i, _):
        sums = [zero] * group
        moments = [zero] * group
        for k in range(length // INNER - 1, -1, -1):
            block = grad_ref[k * INNER : (k + 1) * INNER, :]
            for j in range(group):
                sums[j] = sums[j] + many_ref[i * group + j, k : k + 1, :] * block
                if k > 0:
                    moments[j] = moments[j] + sums[j]
        for j in range(group):
            n = i * group + j
            base = one_ref[n]
            g_ref[pl.ds(n, 1), :] = jnp.sum(base * sums[j], axis=0, keepdims=True)
            m_ref[pl.ds(n, 1), :] = jnp.sum(
                base * (offset * sums[j] + float(INNER) * moments[j]), axis=0, keepdims=True
            )
        return 0

    lax.fori_loop(0, states // group, body, 0)
    rate = rate_ref[0]
    readout = readout_ref[0]
    grad_w = g_ref[...]
    grad_a = -(step * readout) * m_ref[...]
    out_ref[:states, :] = step * grad_a
    out_ref[states : 2 * states, :] = step * grad_w
    out_ref[2 * states :, :] = extra_ref[...]
    out_ref[2 * states : 2 * states + 1, :] = step * jnp.sum(
        readout * grad_w + rate * grad_a, axis=0, keepdims=True
    )


def state_grad(delta, rate, readout, grad, extra, c):
    dirs, states, channels = rate.shape
    length = grad.shape[0]
    lanes = channels // LANES
    spec = pl.BlockSpec((1, states, LANES), lambda j: (c, 0, j))
    row = pl.BlockSpec((1, 1, LANES), lambda j: (c, 0, j))
    rows = 2 * states + extra.shape[0]
    return pl.pallas_call(
        state_grad_kernel,
        name="state_grad",
        grid=(lanes,),
        in_specs=[
            row,
            spec,
            spec,
            pl.BlockSpec((length, LANES), lambda j: (0, c * lanes + j)),
            pl.BlockSpec((extra.shape[0], LANES), lambda j: (0, j)),
        ],
        out_specs=pl.BlockSpec((rows, LANES), lambda j: (0, j)),
        out_shape=jax.ShapeDtypeStruct((rows, channels), F32),
        scratch_shapes=[
            pltpu.VMEM((states, LANES), F32),
            pltpu.VMEM((states, INNER, LANES), F32),
            pltpu.VMEM((states, length // INNER, LANES), F32),
            pltpu.VMEM((states, LANES), F32),
            pltpu.VMEM((states, LANES), F32),
        ],
    )(delta, rate, readout, grad, extra)


def whole(shape):
    return pl.BlockSpec(shape, lambda *at: (0,) * len(shape), pipeline_mode=pl.Buffered(1))


def out(shape):
    return pl.BlockSpec(shape, lambda *at: (0,) * len(shape))


def by_rows(width):
    return pl.BlockSpec((ROWS, width), lambda i, *at: (i, 0))


def response_kernel(first_ref, second_ref, rows_ref, turn_ref, k_ref):
    channels = first_ref.shape[1]
    length = first_ref.shape[0]
    tile = lambda v: jnp.concatenate([v] * (channels // LANES), axis=1)
    c, s = tile(turn_ref[0]), tile(turn_ref[1])
    for i, ref in enumerate((first_ref, second_ref)):
        f = dot_nn(rows_ref[...], ref[...]) * (1.0 / length)
        p, q = f[:BAND], f[BAND:]
        at = slice(i * channels, (i + 1) * channels)
        k_ref[0, 0, :, at] = c * p + s * q
        k_ref[0, 1, :, at] = c * q - s * p


def response(first, second, rows, turn):
    length, channels = first.shape
    bands = length // BAND
    return pl.pallas_call(
        response_kernel,
        name="response",
        grid=(bands,),
        in_specs=[
            whole((length, channels)),
            whole((length, channels)),
            pl.BlockSpec((2 * BAND, length), lambda b: (b, 0)),
            pl.BlockSpec((2, BAND, LANES), lambda b: (0, b, 0)),
        ],
        out_specs=pl.BlockSpec((1, 2, BAND, 2 * channels), lambda b: (b, 0, 0, 0)),
        out_shape=jax.ShapeDtypeStruct((bands, 2, BAND, 2 * channels), F32),
        compiler_params=pltpu.CompilerParams(vmem_limit_bytes=56 << 20),
    )(first, second, rows, turn)


def response_grad_kernel(lag_ref, cols_ref, turn_ref, out_ref):
    length, channels = out_ref.shape
    tile = lambda v: jnp.concatenate([v] * (channels // LANES), axis=1)
    c, s = tile(turn_ref[0]) * (1.0 / length), tile(turn_ref[1]) * (1.0 / length)
    p, q = lag_ref[:BAND], lag_ref[BAND:]
    turned = jnp.concatenate([(c * p - s * q).astype(BF), (s * p + c * q).astype(BF)], axis=0)
    step = dot_nn(cols_ref[...], turned)

    @pl.when(pl.program_id(0) == 0)
    def _():
        out_ref[...] = step

    @pl.when(pl.program_id(0) > 0)
    def _():
        out_ref[...] += step


def response_grad(lag, cols, turn):
    length = cols.shape[0]
    channels = lag.shape[1]
    return pl.pallas_call(
        response_grad_kernel,
        name="response_grad",
        grid=(length // BAND,),
        in_specs=[
            pl.BlockSpec((2 * BAND, channels), lambda b: (b, 0)),
            pl.BlockSpec((length, 2 * BAND), lambda b: (0, b)),
            pl.BlockSpec((2, BAND, LANES), lambda b: (0, b, 0)),
        ],
        out_specs=out((length, channels)),
        out_shape=jax.ShapeDtypeStruct((length, channels), F32),
        compiler_params=pltpu.CompilerParams(vmem_limit_bytes=56 << 20),
    )(lag, cols, turn)


def send_kernel(a_ref, first_ref, second_ref, first_out, second_out):
    first_out[...] = dot_nn(a_ref[...], first_ref[...]).astype(BF)
    second_out[...] = dot_nn(a_ref[...], second_ref[...]).astype(BF)


def send(a, first, second):
    length, width = a.shape
    n = first.shape[1]
    return pl.pallas_call(
        send_kernel,
        name="send",
        grid=(length // ROWS,),
        in_specs=[by_rows(width), whole((width, n)), whole((width, n))],
        out_specs=[by_rows(n), by_rows(n)],
        out_shape=[jax.ShapeDtypeStruct((length, n), BF)] * 2,
    )(a, first, second)


def join_kernel(a_ref, b_ref, add_ref, out_ref):
    out_ref[...] = (dot_nn(a_ref[...], b_ref[...]) + add_ref[...].astype(F32)).astype(BF)


def join(a, b, add):
    length, width = a.shape
    n = b.shape[1]
    return pl.pallas_call(
        join_kernel,
        name="join",
        grid=(length // ROWS,),
        in_specs=[by_rows(width), whole((width, n)), by_rows(n)],
        out_specs=by_rows(n),
        out_shape=jax.ShapeDtypeStruct((length, n), BF),
    )(a, b, add)


def before_gate_kernel(
    slot, length_ref, both_ref, mix_ref, near_ref, mix_bias_ref, normed_ref, value_ref, value_bias_ref,
    cot_ref, out_ref, part_ref, act_ref, first_ref, second_ref, up_ref, sum_ref,
):
    i = pl.program_id(0)
    part_ref[...] = dot_nn(both_ref[...], mix_ref[...]) + near_ref[...].astype(F32) + mix_bias_ref[...]
    act, slope = gelu_pair(dot_nn(normed_ref[...], value_ref[...]) + value_bias_ref[...])
    cot = cot_ref[0].astype(F32)
    time_at = lax.broadcasted_iota(jnp.int32, cot.shape, 0) + i * ROWS
    upstream = jnp.where(time_at < length_ref[slot], cot, 0.0)
    low = upstream.astype(BF)
    grad_hidden = dot_nn(low, out_ref[...])
    act_ref[...] = act
    first_ref[...] = grad_hidden * act
    second_ref[...] = grad_hidden * slope
    up_ref[...] = low

    @pl.when(i == 0)
    def _():
        sum_ref[...] = jnp.zeros_like(sum_ref)

    sum_ref[...] += jnp.sum(upstream, axis=0, keepdims=True)


def before_gate(both, mix, near, mix_bias, normed, last_all, value_bias, cotangent, lengths, slot):
    length, width = normed.shape
    n = mix.shape[1]
    return pl.pallas_call(
        functools.partial(before_gate_kernel, slot),
        name="before_gate",
        grid_spec=pltpu.PrefetchScalarGridSpec(
            num_scalar_prefetch=1,
            grid=(length // ROWS,),
            in_specs=[
                by_rows(both.shape[1]),
                whole(mix.shape),
                by_rows(n),
                whole((1, n)),
                by_rows(width),
                whole((width, n)),
                whole((1, n)),
                pl.BlockSpec((1, ROWS, width), lambda i, *at: (slot, i, 0)),
                pl.BlockSpec((width, n), lambda *at: (0, 1), pipeline_mode=pl.Buffered(1)),
            ],
            out_specs=[by_rows(n)] * 4 + [by_rows(width), out((1, width))],
        ),
        out_shape=[jax.ShapeDtypeStruct((length, n), F32)] * 4
        + [jax.ShapeDtypeStruct((length, width), BF), jax.ShapeDtypeStruct((1, width), F32)],
        compiler_params=pltpu.CompilerParams(vmem_limit_bytes=56 << 20),
    )(lengths, both, mix, near, mix_bias, normed, last_all, value_bias, cotangent, last_all)


def gate_kernel(part_ref, far_ref, act_ref, first_ref, second_ref, hidden_ref, gate_ref, value_ref, sum_ref):
    gate_act, gate_slope = gelu_pair(part_ref[...] + far_ref[...].astype(F32))
    hidden_ref[...] = (gate_act * act_ref[...]).astype(BF)
    gate = (gate_slope * first_ref[...]).astype(BF)
    value = (gate_act * second_ref[...]).astype(BF)
    gate_ref[...] = gate
    value_ref[...] = value

    @pl.when(pl.program_id(0) == 0)
    def _():
        sum_ref[...] = jnp.zeros_like(sum_ref)

    sum_ref[0:1, :] += jnp.sum(gate.astype(F32), axis=0, keepdims=True)
    sum_ref[1:2, :] += jnp.sum(value.astype(F32), axis=0, keepdims=True)


def gate(part, far, act, first, second):
    length, n = part.shape
    return pl.pallas_call(
        gate_kernel,
        name="gate",
        grid=(length // ROWS,),
        in_specs=[by_rows(n)] * 5,
        out_specs=[by_rows(n)] * 3 + [out((2, n))],
        out_shape=[jax.ShapeDtypeStruct((length, n), BF)] * 3 + [jax.ShapeDtypeStruct((2, n), F32)],
        compiler_params=pltpu.CompilerParams(vmem_limit_bytes=56 << 20),
    )(part, far, act, first, second)


def tables(length):
    odd = 2 * np.arange(length, dtype=np.int64) + 1
    angle = (odd[:, None] * odd[None, :]) % (8 * length) * (math.pi / (4 * length))
    bands = length // BAND
    both = np.stack([np.cos(angle).reshape(bands, BAND, length), np.sin(angle).reshape(bands, BAND, length)], axis=1)
    rows = both.reshape(2 * length, length)
    turn = odd * (math.pi / (4 * length))
    return rows.astype(BF), np.ascontiguousarray(rows.T).astype(BF), np.repeat(
        np.stack([np.cos(turn), np.sin(turn)])[:, :, None], LANES, axis=2
    ).astype(np.float32)

def gate_weight_kernel(lefts, count, side_ref, *refs):
    left_refs, right_refs, (give_ref, keep_ref) = refs[:lefts], refs[lefts:-2], refs[-2:]
    for j in range(count):

        @pl.when(pl.program_id(1) == j)
        def _():
            pieces = right_refs[j * lefts : (j + 1) * lefts]
            total = dot_tn(left_refs[0][...], pieces[0][...])
            for left, piece in zip(left_refs[1:], pieces[1:]):
                total = total + dot_tn(left[...], piece[...])

            @pl.when(pl.program_id(0) == 0)
            def _():
                give_ref[0] = total.astype(BF)

            @pl.when(pl.program_id(0) == 1)
            def _():
                keep_ref[0] = total


def gate_weight(left, quarters, side):
    length, rows = left[0].shape
    count = len(quarters)
    cols = quarters[0][0].shape[1] // 2
    half = pl.BlockSpec((length, cols), lambda w, j, side: (0, jnp.where(w == 0, 1 - side[0], side[0])))
    return pl.pallas_call(
        functools.partial(gate_weight_kernel, len(left), count),
        name="gate_weight",
        grid_spec=pltpu.PrefetchScalarGridSpec(
            num_scalar_prefetch=1,
            grid=(2, count),
            in_specs=[whole((length, rows))] * len(left) + [half] * (count * len(left)),
            out_specs=[
                pl.BlockSpec((1, rows, cols), lambda w, j, side: (jnp.where(w == 0, j, count - 1), 0, 0)),
                pl.BlockSpec((1, rows, cols), lambda w, j, side: (jnp.where(w == 0, 0, j), 0, 0)),
            ],
        ),
        out_shape=[
            jax.ShapeDtypeStruct((count, rows, cols), BF),
            jax.ShapeDtypeStruct((count, rows, cols), F32),
        ],
        compiler_params=pltpu.CompilerParams(vmem_limit_bytes=56 << 20),
    )(side, *left, *[piece for quarter in quarters for piece in quarter])


def row_weight_kernel(slots, side_ref, *refs):
    left_refs, right_refs, (give_ref, keep_ref) = refs[: 2 * slots], refs[2 * slots : -2], refs[-2:]
    for j in range(2):

        @pl.when(pl.program_id(1) == j)
        def _():
            lefts = left_refs[j * slots : (j + 1) * slots]
            rights = right_refs[j * slots : (j + 1) * slots]
            total = dot_tn(lefts[0][...], rights[0][...])
            for left, right in zip(lefts[1:], rights[1:]):
                total = total + dot_tn(left[...], right[...])

            @pl.when(pl.program_id(0) == 0)
            def _():
                give_ref[...] = total.astype(BF)

            @pl.when(pl.program_id(0) == 1)
            def _():
                keep_ref[...] = total


def row_weight(pairs, side):
    slots = len(pairs[0][0])
    length, rows = pairs[0][0][0].shape
    cols = pairs[0][1][0].shape[1]
    half = pl.BlockSpec((length, rows // 2), lambda w, j, side: (0, jnp.where(w == 0, 1 - side[0], side[0])))
    return pl.pallas_call(
        functools.partial(row_weight_kernel, slots),
        name="row_weight",
        grid_spec=pltpu.PrefetchScalarGridSpec(
            num_scalar_prefetch=1,
            grid=(2, 2),
            in_specs=[half] * (2 * slots) + [whole((length, cols))] * (2 * slots),
            out_specs=[
                pl.BlockSpec((rows // 2, cols), lambda w, j, side: (0, jnp.where(w == 0, j, 1))),
                pl.BlockSpec((rows // 2, cols), lambda w, j, side: (0, jnp.where(w == 0, 0, j))),
            ],
        ),
        out_shape=[
            jax.ShapeDtypeStruct((rows // 2, 2 * cols), BF),
            jax.ShapeDtypeStruct((rows // 2, 2 * cols), F32),
        ],
        compiler_params=pltpu.CompilerParams(vmem_limit_bytes=56 << 20),
    )(side, *pairs[0][0], *pairs[1][0], *pairs[0][1], *pairs[1][1])


def conv_forward_kernel(slot, length_ref, normed_ref, weight_ref, bias_ref, rows_ref, cols_ref, k_ref, skip_ref, slope_ref, low_ref, u_ref, both_ref, total_ref):
    band = pl.program_id(0)
    length, channels = slope_ref.shape

    @pl.when(band == 0)
    def _():
        def body(i, _):
            at = pl.ds(pl.multiple_of(i * 256, 256), 256)
            pre = dot_nn(normed_ref[at, :], weight_ref[...]) + bias_ref[...]
            value, slope = gelu_pair(pre)
            time_at = lax.broadcasted_iota(jnp.int32, pre.shape, 0) + i * 256
            live = jnp.where(time_at < length_ref[slot], 1.0, 0.0)
            signal = value * live
            slope_ref[at, :] = slope * live
            low_ref[at, :] = signal.astype(BF)
            total_ref[at, :channels] = skip_ref[0:1, :] * signal
            total_ref[at, channels:] = skip_ref[1:2, :] * signal
            return 0
        lax.fori_loop(0, length // 256, body, 0)

    u = dot_nn(rows_ref[...], low_ref[...])
    u_ref[...] = u
    uc, us = u[:BAND], u[BAND:]
    k0c, k1c = k_ref[0, 0, :, :channels], k_ref[0, 0, :, channels:]
    k0s, k1s = k_ref[0, 1, :, :channels], k_ref[0, 1, :, channels:]
    product = jnp.concatenate(
        [
            jnp.concatenate([uc * k0c - us * k0s, uc * k1c + us * k1s], axis=1).astype(BF),
            jnp.concatenate([uc * k0s + us * k0c, us * k1c - uc * k1s], axis=1).astype(BF),
        ],
        axis=0,
    )
    total_ref[...] += dot_nn(cols_ref[...], product)

    @pl.when(band == pl.num_programs(0) - 1)
    def _():
        both_ref[...] = total_ref[...].astype(BF)

def conv_forward(normed, weight, bias, k, skip, lengths, rows, cols, slot):
    length, width = normed.shape
    channels = weight.shape[1]
    bands = length // BAND
    return pl.pallas_call(
        functools.partial(conv_forward_kernel, slot),
        name="conv_forward",
        grid_spec=pltpu.PrefetchScalarGridSpec(
            num_scalar_prefetch=1,
            grid=(bands,),
            in_specs=[
                whole((length, width)), whole((width, channels)), whole((1, channels)),
                pl.BlockSpec((2 * BAND, length), lambda b, n: (b, 0)),
                pl.BlockSpec((length, 2 * BAND), lambda b, n: (0, b)),
                pl.BlockSpec((1, 2, BAND, 2 * channels), lambda b, n: (b, 0, 0, 0)),
                whole((2, channels)),
            ],
            out_specs=[
                out((length, channels)), out((length, channels)),
                pl.BlockSpec((2 * BAND, channels), lambda b, n: (b, 0)),
                out((length, 2 * channels)),
            ],
            scratch_shapes=[pltpu.VMEM((length, 2 * channels), F32)],
        ),
        out_shape=[
            jax.ShapeDtypeStruct((length, channels), F32),
            jax.ShapeDtypeStruct((length, channels), BF),
            jax.ShapeDtypeStruct((2 * length, channels), F32),
            jax.ShapeDtypeStruct((length, 2 * channels), BF),
        ],
        compiler_params=pltpu.CompilerParams(vmem_limit_bytes=56 << 20),
    )(lengths, normed, weight, bias, rows, cols, k, skip)

def conv_backward_kernel(count, *refs):
    pieces, mixes = refs[:count], refs[count:2 * count]
    rows_ref, cols_ref, k_ref, u_ref, slope_ref, low_ref, skip_ref, before_ref, feed_ref, lag_ref, skips_ref, both_ref, total_ref = refs[2 * count:]
    band = pl.program_id(0)
    length, channels = slope_ref.shape

    blocks = length // ROWS

    @pl.when(band == 0)
    def _():
        skips_ref[...] = jnp.zeros_like(skips_ref)

    @pl.when(band < blocks)
    def _():
        at = pl.ds(pl.multiple_of(band * ROWS, ROWS), ROWS)
        both = dot_nt(pieces[0][...], mixes[0][...])
        for piece, mix in zip(pieces[1:], mixes[1:]):
            both = both + dot_nt(piece[...], mix[...])
        both_ref[at, :] = both.astype(BF)
        total_ref[at, :] = skip_ref[0:1, :] * both[:, :channels] + skip_ref[1:2, :] * both[:, channels:]
        signal = low_ref[...].astype(F32)
        skips_ref[...] += jnp.sum(both * jnp.concatenate([signal, signal], axis=1), axis=0, keepdims=True)

    @pl.when(band >= blocks)
    def _():
        conv_backward_band(
            rows_ref, cols_ref, k_ref, u_ref, before_ref, lag_ref, both_ref, total_ref, channels
        )

    @pl.when(band == pl.num_programs(0) - 1)
    def _():
        feed_ref[...] = (slope_ref[...] * total_ref[...]).astype(BF)


def conv_backward_band(rows_ref, cols_ref, k_ref, u_ref, before_ref, lag_ref, both_ref, total_ref, channels):
    g = dot_nn(rows_ref[...], both_ref[...])
    ac, bc = g[:BAND, :channels], g[:BAND, channels:]
    as_, bs = g[BAND:, :channels], g[BAND:, channels:]
    uc, us = u_ref[:BAND], u_ref[BAND:]
    k0c, k1c = k_ref[0, 0, :, :channels], k_ref[0, 0, :, channels:]
    k0s, k1s = k_ref[0, 1, :, :channels], k_ref[0, 1, :, channels:]
    back = jnp.concatenate(
        [
            (ac * k0c + as_ * k0s + bc * k1c - bs * k1s).astype(BF),
            (as_ * k0c - ac * k0s + bc * k1s + bs * k1c).astype(BF),
        ],
        axis=0,
    )
    if before_ref is None:
        lag_ref[:BAND, :channels] = ac * uc + as_ * us
        lag_ref[:BAND, channels:] = uc * bc + us * bs
        lag_ref[BAND:, :channels] = as_ * uc - ac * us
        lag_ref[BAND:, channels:] = us * bc - uc * bs
    else:
        lag_ref[:BAND, :channels] = before_ref[:BAND, :channels] + ac * uc + as_ * us
        lag_ref[:BAND, channels:] = before_ref[:BAND, channels:] + uc * bc + us * bs
        lag_ref[BAND:, :channels] = before_ref[BAND:, :channels] + as_ * uc - ac * us
        lag_ref[BAND:, channels:] = before_ref[BAND:, channels:] + us * bc - uc * bs
    total_ref[...] += dot_nn(cols_ref[...], back)

def conv_backward(pieces, mixes, k, u, slope, low, skip, rows, cols, before):
    length, channels = slope.shape
    width = pieces[0].shape[1]
    bands = length // BAND
    blocks = length // ROWS
    band = lambda b: jnp.maximum(b - blocks, 0)
    band_spec = pl.BlockSpec((2 * BAND, 2 * channels), lambda b: (band(b), 0))
    streamed = lambda n: pl.BlockSpec((ROWS, n), lambda b: (jnp.minimum(b, blocks - 1), 0))
    count = len(pieces)
    def kernel(*refs):
        at = 2 * count + 7
        if before is None: refs = refs[:at] + (None,) + refs[at:]
        conv_backward_kernel(count, *refs)
    return pl.pallas_call(
        kernel,
        name="conv_backward",
        grid=(blocks + bands,),
        in_specs=[streamed(width)] * count + [whole((2 * channels, width))] * count + [
            pl.BlockSpec((2 * BAND, length), lambda b: (band(b), 0)),
            pl.BlockSpec((length, 2 * BAND), lambda b: (0, band(b))),
            pl.BlockSpec((1, 2, BAND, 2 * channels), lambda b: (band(b), 0, 0, 0)),
            pl.BlockSpec((2 * BAND, channels), lambda b: (band(b), 0)),
            whole((length, channels)), streamed(channels), whole((2, channels)),
        ] + ([] if before is None else [band_spec]),
        out_specs=[out((length, channels)), band_spec, out((1, 2 * channels))],
        out_shape=[
            jax.ShapeDtypeStruct((length, channels), BF),
            jax.ShapeDtypeStruct((2 * length, 2 * channels), F32),
            jax.ShapeDtypeStruct((1, 2 * channels), F32),
        ],
        scratch_shapes=[pltpu.VMEM((length, 2 * channels), BF), pltpu.VMEM((length, channels), F32)],
        compiler_params=pltpu.CompilerParams(vmem_limit_bytes=60 << 20),
    )(*pieces, *mixes, rows, cols, k, u, slope, low, skip, *(() if before is None else (before,)))


def make_shards(dp_size, tensor_size):
    core_swap = [(i, i ^ 1) for i in range(tensor_size)]
    far_swap = [(i, i ^ 2) for i in range(tensor_size)]
    parts_of = dp_size // tensor_size

    def near(v):
        return lax.ppermute(v, "tensor", core_swap)

    def far(v):
        return lax.ppermute(v, "tensor", far_swap)

    def across(v, mask):
        return lax.ppermute(v, "dp", [(i, i ^ mask) for i in range(dp_size)])

    def shards(
        inputs,
        cotangent,
        lengths,
        norm_gain,
        norm_bias,
        value_weight,
        value_bias,
        feed_weight,
        feed_bias,
        mix_forward,
        mix_backward,
        mix_bias,
        out_weight,
        out_bias,
        state_delta,
        state_rate,
        state_readout,
        state_skip,
    ):
        slots, length, width = inputs.shape
        channels = feed_weight.shape[1]
        hidden_width = value_weight.shape[1]
        states = state_rate.shape[2]
        me = lax.axis_index("tensor")
        rank = lax.axis_index("dp")
        core = me % 2
        half = length // 2

        def collect(v):
            whole_v = v[None]
            mask = dp_size // 2
            stages = []
            while mask:
                stages.append(whole_v)
                other = across(whole_v, mask)
                upper = (rank & mask) != 0
                whole_v = jnp.stack(
                    [jnp.where(upper, other, whole_v), jnp.where(upper, whole_v, other)], axis=1
                )
                whole_v = whole_v.reshape((-1,) + v.shape)
                mask //= 2
            return whole_v.reshape((-1,) + v.shape[1:]), stages

        class Halving:
            def __init__(self, blocks):
                self.blocks = blocks
                self.give = None

            def send(self, give, keep, mask):
                self.give, self.blocks = give, keep
                self.got = across(give, mask)
                return self

            def launch(self, mask, flip=False):
                upper = ((rank & mask) != 0) ^ flip
                pairs = list(zip(self.blocks[::2], self.blocks[1::2]))
                self.give = jnp.concatenate(
                    [jnp.where(upper, a, b).astype(BF) for a, b in pairs], axis=0
                )
                self.blocks = [jnp.where(upper, b, a) for a, b in pairs]
                self.got = across(self.give, mask)
                return self

            def land(self, *anchors):
                got = after(self.got, *anchors)
                size = self.blocks[0].shape[0]
                self.blocks = [
                    b + got[i * size : (i + 1) * size].astype(F32) for i, b in enumerate(self.blocks)
                ]
                return self

        def row_blocks(v, count):
            size = v.shape[0] // count
            return [v[i * size : (i + 1) * size] for i in range(count)]

        def side(mask):
            return ((rank & mask) != 0).astype(jnp.int32).reshape(1)

        def total_over_dp(v):
            mask = 1
            while mask < dp_size:
                v = v + across(v, mask)
                mask *= 2
            return v

        feed_full, feed_stages = collect(feed_weight)
        mix_own = jnp.concatenate([mix_forward, mix_backward], axis=0)
        mix_all = lax.all_gather(mix_own, "dp", axis=0, tiled=False)
        last_own = jnp.concatenate([value_weight, out_weight.T], axis=1)
        last_all = lax.all_gather(last_own, "dp", axis=0, tiled=True)

        delta = state_delta[:, None, :]
        rate = jnp.swapaxes(state_rate, 1, 2)
        readout = jnp.swapaxes(state_readout, 1, 2)
        fourier_rows, fourier_cols, turn = (jnp.asarray(v) for v in tables(length))
        pulses = [
            impulse(after(delta, feed_stages[c - 2]), rate, readout, length, c) for c in range(2)
        ]
        spectra = response(pulses[0], pulses[1], fourier_rows, turn)

        time_at = jnp.arange(length)[:, None]
        normed, slope, low, u, both = [], [], [], [], []
        for slot in range(slots):
            rows = inputs[slot].astype(F32)
            center = rows - jnp.mean(rows, axis=-1, keepdims=True)
            spread = jnp.mean(center * center, axis=-1, keepdims=True)
            normed.append((center * lax.rsqrt(spread + EPSILON) * norm_gain + norm_bias).astype(BF))
        for slot in range(slots):
            parts = conv_forward(
                normed[slot],
                feed_full,
                feed_bias[None, :],
                spectra,
                state_skip,
                lengths,
                fourier_rows,
                fourier_cols,
                slot,
            )
            for whole_list, part in zip((slope, low, u, both), parts):
                whole_list.append(part)

        mix_all = after(mix_all, *both)
        mix_groups = mix_all.reshape((tensor_size, parts_of) + mix_own.shape)
        mix_of = []
        for j in range(tensor_size):
            quarter = lax.dynamic_index_in_dim(mix_groups, me ^ j, axis=0, keepdims=False)
            mix_of.append(jnp.concatenate([quarter[i] for i in range(parts_of)], axis=1))

        passed = None
        near_own, passes = [], []
        for slot in range(slots):
            left = both[slot] if passed is None else after(both[slot], passed)
            to_own, to_pass = send(left, mix_of[1], mix_of[3])
            passed = join(left, mix_of[2], near(to_pass))
            near_own.append(near(to_own))
            passes.append(passed)
        last_all = after(last_all, passed)
        pre = []
        for slot in range(slots):
            pre.append(
                before_gate(
                    both[slot],
                    mix_of[0],
                    near_own[slot],
                    mix_bias[None, :],
                    normed[slot],
                    last_all,
                    value_bias[None, :],
                    cotangent,
                    lengths,
                    slot,
                )
            )
        upstream_low = [p[4] for p in pre]
        value_full = last_all[:, :hidden_width]
        out_all = last_all[:, hidden_width:]

        hidden, grad_gate, grad_value, gate_sums = [], [], [], []
        for slot in range(slots):
            arrived = far(passes[slot])
            if slot == 0:
                arrived = after(arrived, pre[-1][0])
            else:
                arrived = after(arrived, grad_gate[-1])
            parts = gate(pre[slot][0], arrived, *pre[slot][1:4])
            for whole_list, part in zip((hidden, grad_gate, grad_value, gate_sums), parts):
                whole_list.append(part)
        far_gate = [far(g) for g in grad_gate]
        near_gate = [near(g) for g in grad_gate]

        top = dp_size // 2
        give, keep = row_weight(((normed, grad_value), (upstream_low, hidden)), side(top))
        last_sum = Halving(None).send(give, [keep], top)

        def next_rows(halving, mask, *anchors):
            halving.land(*anchors)
            halving.blocks = row_blocks(halving.blocks[0], 2)
            return halving.launch(mask)

        first = core == 0
        branches = [dot_nt(hidden[slot], out_all) for slot in range(slots)]
        branch_keep = jnp.where(first, branches[0], branches[1])
        branch_give = jnp.where(first, branches[1], branches[0]).astype(BF)

        low_masks = [1 << i for i in range(parts_of.bit_length() - 1)]

        def start_low(quarters):
            quarters = [[after(piece, last_sum.give) for piece in quarter] for quarter in quarters]
            if parts_of == 2:
                give, keep = gate_weight(both, quarters, side(1))
                return Halving(None).send(give.reshape(-1, give.shape[2]), [keep[0], keep[1]], 1)
            size = hidden_width // parts_of
            blocks = []
            for quarter in quarters:
                g = sum(dot_tn(b, piece) for b, piece in zip(both, quarter))
                blocks += [g[:, i * size : (i + 1) * size] for i in range(parts_of)]
            return Halving(blocks).launch(low_masks[0])

        def finish_low(halving, *anchors):
            for mask in low_masks[1:]:
                halving.land(*anchors).launch(mask)
            return halving.land(*anchors).launch(parts_of, core == 1)

        near_sum = start_low([grad_gate, near_gate])
        branch_pair = (branch_keep + near(branch_give).astype(F32)).astype(BF)

        early = [sum(g[0:1] for g in gate_sums), sum(g[1:2] for g in gate_sums), sum(p[5] for p in pre)]

        def back(slot, arrived, lag, *anchors):
            pieces = [grad_gate[slot], near_gate[slot], arrived, near(arrived)]
            pieces[0] = after(pieces[0], *anchors)
            return pieces[3], conv_backward(
                pieces,
                mix_of,
                spectra,
                u[slot],
                slope[slot],
                low[slot],
                state_skip,
                fourier_rows,
                fourier_cols,
                lag,
            )

        def features(slot, grad_feed):
            v = dot_nt(grad_value[slot], value_full) + dot_nt(grad_feed, feed_full)
            give = lax.dynamic_slice_in_dim(v, (1 - core) * half, half, 0).astype(BF)
            keep = lax.dynamic_slice_in_dim(v, core * half, half, 0)
            return give, keep

        arrived_a = after(far_gate[0], last_sum.give)
        far_near_a, (grad_feed_a, lag, skips_a) = back(
            0, arrived_a, None, near_sum.give, last_sum.give, branch_pair
        )
        give_a, keep_a = features(0, grad_feed_a)
        near_a = near(give_a)
        masks = [top >> i for i in range(1, top.bit_length())]
        next_rows(last_sum, masks[0], grad_feed_a)
        near_sum = finish_low(near_sum, grad_feed_a)

        arrived_b = after(far_gate[1], last_sum.give, near_sum.give, give_a)
        far_near_b = near(arrived_b)
        far_sum = start_low([[arrived_a, arrived_b], [far_near_a, far_near_b]])
        pair_a = (keep_a + near_a.astype(F32)).astype(BF)
        far_near_b, (grad_feed_b, lag, skips_b) = back(1, arrived_b, lag, far_sum.give, pair_a)
        far_a = far(pair_a)
        for mask in masks[1:]:
            next_rows(last_sum, mask, grad_feed_b)
        give_b, keep_b = features(1, grad_feed_b)
        near_b = near(give_b)
        near_sum.land(grad_feed_b)
        far_sum = finish_low(far_sum, give_b)

        feed_sum = Halving(
            row_blocks(dot_tn(normed[0], grad_feed_a) + dot_tn(normed[1], grad_feed_b), 2)
        ).launch(top)
        feed_bias_sum = jnp.sum(grad_feed_a.astype(F32), axis=0, keepdims=True) + jnp.sum(
            grad_feed_b.astype(F32), axis=0, keepdims=True
        )
        grad_response = response_grad(after(lag, give_b, far_sum.give, feed_sum.give), fourier_cols, turn)
        pair_b = (keep_b + after(near_b, grad_response).astype(F32)).astype(BF)
        far_b = far(pair_b)

        def state_step(c, *anchors):
            at = slice(c * channels, (c + 1) * channels)
            extra = [skips_a[:, at], skips_a[:, at] + skips_b[:, at]] + [v[:, at] for v in early]
            extra += [feed_bias_sum] * 3
            return state_grad(
                delta, rate, readout, after(grad_response, *anchors), jnp.concatenate(extra, axis=0), c
            )

        def finish_rows(slot, pair, arrived):
            total = pair.astype(F32) + arrived.astype(F32)
            rows = lax.dynamic_slice_in_dim(inputs[slot], core * half, half, 0).astype(F32)
            up_half = lax.dynamic_slice_in_dim(upstream_low[slot], core * half, half, 0).astype(F32)
            center = rows - jnp.mean(rows, axis=-1, keepdims=True)
            spread = jnp.mean(center * center, axis=-1, keepdims=True)
            inverse = lax.rsqrt(spread + EPSILON)
            unit = center * inverse
            weighted = total * norm_gain
            mine = (
                up_half
                + (
                    weighted
                    - jnp.mean(weighted, axis=-1, keepdims=True)
                    - unit * jnp.mean(weighted * unit, axis=-1, keepdims=True)
                )
                * inverse
            ).astype(BF)
            sums = jnp.concatenate(
                [jnp.sum(total * unit, axis=0, keepdims=True), jnp.sum(total, axis=0, keepdims=True)], axis=0
            )
            return mine, sums

        masks_up = [1 << i for i in range(dp_size.bit_length() - 1)]
        state_a = state_step(0, pair_b)
        sent = across(state_a, masks_up[0])
        far_sum.land(state_a)
        mix_sum = Halving([near_sum.blocks[0], far_sum.blocks[0]]).launch(2 * parts_of, me >= 2)
        next_rows(feed_sum, masks[0], state_a)

        rows = jnp.where(first, inputs[0], inputs[1]).astype(F32)
        live = (time_at < jnp.where(first, lengths[0], lengths[1])).astype(F32)
        branch_far = after(far(branch_pair), state_a)
        mine = (live * (rows + (branch_pair.astype(F32) + branch_far.astype(F32)) + out_bias)).astype(BF)
        theirs = near(mine)
        rows_a, norm_a = finish_rows(0, pair_a, after(far_a, state_a))
        state_a = state_a + after(sent, rows_a, mine)
        sent = across(state_a, masks_up[1])
        state_b = state_step(1, state_a, mix_sum.give, feed_sum.give, theirs)
        layer_out = jnp.stack([jnp.where(first, mine, theirs), jnp.where(first, theirs, mine)])
        state_a = state_a + after(sent, state_b)
        sent_b = across(state_b, masks_up[0])
        for mask in masks_up[2:]:
            sent = across(state_a, mask)
            state_a = state_a + (after(sent, layer_out) if mask < top else sent)
        rows_b, norm_b = finish_rows(1, pair_b, after(far_b, state_b))
        mine = jnp.stack([rows_a, rows_b])
        theirs = near(mine)
        state_b = state_b + after(sent_b, rows_b)
        sent_b = across(state_b, masks_up[1])
        for i, mask in enumerate(masks[1:]):
            next_rows(feed_sum, mask, *((rows_b,) if i == 0 else ()))
        small = after(norm_a + norm_b, state_b)
        small_sent = across(small, masks_up[0])
        last_sum = last_sum.land(state_b).blocks[0]
        state_b = state_b + after(sent_b, last_sum)
        sent_b = across(state_b, masks_up[2])
        small = small + after(small_sent, state_b)
        small_sent = across(small, masks_up[1])
        mix_sum = mix_sum.land(state_b).blocks[0]
        theirs = after(theirs, mix_sum)
        input_grad = jnp.concatenate([jnp.where(first, mine, theirs), jnp.where(first, theirs, mine)], axis=1)
        small = small + after(small_sent, mix_sum)
        small_sent = across(small, masks_up[2])
        feed_sum = feed_sum.land(mix_sum).blocks[0]
        state_b = state_b + after(sent_b, input_grad)
        small = small + small_sent
        for mask in masks_up[3:]:
            state_b = state_b + across(state_b, mask)
            small = small + across(small, mask)
        norm_sums = small + near(small)
        totals = jnp.stack([state_a, state_b])
        tail_rows = totals[:, 2 * states :]
        early = [tail_rows[:, i].reshape(-1) for i in (2, 3, 4)]

        return (
            layer_out,
            input_grad,
            norm_sums[0],
            norm_sums[1],
            last_sum[:, :hidden_width],
            early[1],
            feed_sum,
            tail_rows[0, 5],
            mix_sum[:channels],
            mix_sum[channels:],
            early[0],
            last_sum[:, hidden_width:].T,
            early[2],
            tail_rows[:, 0],
            jnp.swapaxes(totals[:, :states], 1, 2),
            jnp.swapaxes(totals[:, states : 2 * states], 1, 2),
            tail_rows[:, 1],
        )

    return shards


def solution(mesh):
    placed = (
        P("dp", None, None),
        P("dp", None, None),
        P("dp"),
        P(),
        P(),
        P("dp", "tensor"),
        P("tensor"),
        P("dp", "tensor"),
        P("tensor"),
        P("tensor", "dp"),
        P("tensor", "dp"),
        P("tensor"),
        P("tensor", "dp"),
        P(),
        P(None, "tensor"),
        P(None, "tensor", None),
        P(None, "tensor", None),
        P(None, "tensor"),
    )
    return jax.shard_map(
        make_shards(mesh.shape["dp"], mesh.shape["tensor"]),
        mesh=mesh,
        in_specs=placed,
        out_specs=(
            P("dp", None, None),
            P("dp", None, None),
            P(),
            P(),
            P("dp", "tensor"),
            P("tensor"),
            P("dp", "tensor"),
            P("tensor"),
            P("tensor", "dp"),
            P("tensor", "dp"),
            P("tensor"),
            P("tensor", "dp"),
            P(),
            P(None, "tensor"),
            P(None, "tensor", None),
            P(None, "tensor", None),
            P(None, "tensor"),
        ),
        check_vma=False,
    )
```

```python
import functools
import math

import jax
import jax.numpy as jnp
import numpy as np
from jax import lax
from jax.experimental import pallas as pl
from jax.experimental.pallas import tpu as pltpu
from jax.sharding import PartitionSpec as P

EPSILON = 1e-05
LANES = 128
INNER = 32
BAND = 256
ROWS = 256
BF = jnp.bfloat16
F32 = jnp.float32
GELU_C = math.sqrt(2.0 / math.pi)
GELU_A = 0.044715


def gelu_pair(x):
    square = x * x
    bend = jnp.tanh(GELU_C * x * (1.0 + GELU_A * square))
    half = 0.5 * (1.0 + bend)
    slope = half + 0.5 * x * (1.0 - bend * bend) * (GELU_C * (1.0 + 3.0 * GELU_A * square))
    return x * half, slope


def after(value, *others):
    return lax.optimization_barrier((value,) + others)[0]


def dot_nt(a, b):
    return lax.dot_general(a, b, (((1,), (1,)), ((), ())), preferred_element_type=F32)


def dot_tn(a, b):
    return lax.dot_general(a, b, (((0,), (0,)), ((), ())), preferred_element_type=F32)


def dot_nn(a, b):
    return jnp.dot(a, b, preferred_element_type=F32)


def fill_powers(rate_ref, one_ref, many_ref, scale):
    states = rate_ref.shape[0]
    offset = lax.broadcasted_iota(jnp.int32, (INNER, LANES), 0).astype(F32)

    def body(n, _):
        row = rate_ref[pl.ds(n, 1), :]
        one_ref[n] = jnp.exp(-(row * offset))
        wide = jnp.exp(-(row * (offset * float(INNER))))
        if scale is not None:
            wide = wide * scale[pl.ds(n, 1), :]
        many_ref[n] = wide
        return 0

    lax.fori_loop(0, states, body, 0, unroll=8)


def impulse_kernel(delta_ref, rate_ref, readout_ref, out_ref, a_ref, w_ref, one_ref, many_ref):
    states = rate_ref.shape[1]
    length = out_ref.shape[0]
    step = jnp.exp(delta_ref[0])
    a_ref[...] = step * rate_ref[0]
    w_ref[...] = step * readout_ref[0]
    fill_powers(a_ref, one_ref, many_ref, w_ref)
    group = 8
    for start in range(0, length // INNER, group):

        def body(n, sums):
            base = one_ref[n]
            return tuple(
                total + many_ref[n, start + j : start + j + 1, :] * base
                for j, total in enumerate(sums)
            )

        sums = lax.fori_loop(
            0, states, body, tuple(jnp.zeros((INNER, LANES), F32) for _ in range(group)), unroll=8
        )
        for j, total in enumerate(sums):
            at = (start + j) * INNER
            out_ref[at : at + INNER, :] = total.astype(out_ref.dtype)


def impulse(delta, rate, readout, length, c):
    dirs, states, channels = rate.shape
    lanes = channels // LANES
    spec = pl.BlockSpec((1, states, LANES), lambda j: (c, 0, j))
    return pl.pallas_call(
        impulse_kernel,
        name="impulse",
        grid=(lanes,),
        in_specs=[pl.BlockSpec((1, 1, LANES), lambda j: (c, 0, j)), spec, spec],
        out_specs=pl.BlockSpec((length, LANES), lambda j: (0, j)),
        out_shape=jax.ShapeDtypeStruct((length, channels), BF),
        scratch_shapes=[
            pltpu.VMEM((states, LANES), F32),
            pltpu.VMEM((states, LANES), F32),
            pltpu.VMEM((states, INNER, LANES), F32),
            pltpu.VMEM((states, length // INNER, LANES), F32),
        ],
    )(delta, rate, readout)


def state_grad_kernel(
    delta_ref, rate_ref, readout_ref, grad_ref, extra_ref, out_ref, a_ref, one_ref, many_ref, g_ref, m_ref
):
    states = rate_ref.shape[1]
    length = grad_ref.shape[0]
    step = jnp.exp(delta_ref[0])
    a_ref[...] = step * rate_ref[0]
    fill_powers(a_ref, one_ref, many_ref, None)
    offset = lax.broadcasted_iota(jnp.int32, (INNER, LANES), 0).astype(F32)
    group = 4
    zero = jnp.zeros((INNER, LANES), F32)

    def body(i, _):
        sums = [zero] * group
        moments = [zero] * group
        for k in range(length // INNER - 1, -1, -1):
            block = grad_ref[k * INNER : (k + 1) * INNER, :]
            for j in range(group):
                sums[j] = sums[j] + many_ref[i * group + j, k : k + 1, :] * block
                if k > 0:
                    moments[j] = moments[j] + sums[j]
        for j in range(group):
            n = i * group + j
            base = one_ref[n]
            g_ref[pl.ds(n, 1), :] = jnp.sum(base * sums[j], axis=0, keepdims=True)
            m_ref[pl.ds(n, 1), :] = jnp.sum(
                base * (offset * sums[j] + float(INNER) * moments[j]), axis=0, keepdims=True
            )
        return 0

    lax.fori_loop(0, states // group, body, 0)
    rate = rate_ref[0]
    readout = readout_ref[0]
    grad_w = g_ref[...]
    grad_a = -(step * readout) * m_ref[...]
    out_ref[:states, :] = step * grad_a
    out_ref[states : 2 * states, :] = step * grad_w
    out_ref[2 * states :, :] = extra_ref[...]
    out_ref[2 * states : 2 * states + 1, :] = step * jnp.sum(
        readout * grad_w + rate * grad_a, axis=0, keepdims=True
    )


def state_grad(delta, rate, readout, grad, extra, c):
    dirs, states, channels = rate.shape
    length = grad.shape[0]
    lanes = channels // LANES
    spec = pl.BlockSpec((1, states, LANES), lambda j: (c, 0, j))
    row = pl.BlockSpec((1, 1, LANES), lambda j: (c, 0, j))
    rows = 2 * states + extra.shape[0]
    return pl.pallas_call(
        state_grad_kernel,
        name="state_grad",
        grid=(lanes,),
        in_specs=[
            row,
            spec,
            spec,
            pl.BlockSpec((length, LANES), lambda j: (0, c * lanes + j)),
            pl.BlockSpec((extra.shape[0], LANES), lambda j: (0, j)),
        ],
        out_specs=pl.BlockSpec((rows, LANES), lambda j: (0, j)),
        out_shape=jax.ShapeDtypeStruct((rows, channels), F32),
        scratch_shapes=[
            pltpu.VMEM((states, LANES), F32),
            pltpu.VMEM((states, INNER, LANES), F32),
            pltpu.VMEM((states, length // INNER, LANES), F32),
            pltpu.VMEM((states, LANES), F32),
            pltpu.VMEM((states, LANES), F32),
        ],
    )(delta, rate, readout, grad, extra)


def whole(shape):
    return pl.BlockSpec(shape, lambda *at: (0,) * len(shape), pipeline_mode=pl.Buffered(1))


def out(shape):
    return pl.BlockSpec(shape, lambda *at: (0,) * len(shape))


def by_rows(width):
    return pl.BlockSpec((ROWS, width), lambda i, *at: (i, 0))


def response_kernel(first_ref, second_ref, rows_ref, turn_ref, k_ref):
    channels = first_ref.shape[1]
    length = first_ref.shape[0]
    tile = lambda v: jnp.concatenate([v] * (channels // LANES), axis=1)
    c, s = tile(turn_ref[0]), tile(turn_ref[1])
    for i, ref in enumerate((first_ref, second_ref)):
        f = dot_nn(rows_ref[...], ref[...]) * (1.0 / length)
        p, q = f[:BAND], f[BAND:]
        at = slice(i * channels, (i + 1) * channels)
        k_ref[0, 0, :, at] = c * p + s * q
        k_ref[0, 1, :, at] = c * q - s * p


def response(first, second, rows, turn):
    length, channels = first.shape
    bands = length // BAND
    return pl.pallas_call(
        response_kernel,
        name="response",
        grid=(bands,),
        in_specs=[
            whole((length, channels)),
            whole((length, channels)),
            pl.BlockSpec((2 * BAND, length), lambda b: (b, 0)),
            pl.BlockSpec((2, BAND, LANES), lambda b: (0, b, 0)),
        ],
        out_specs=pl.BlockSpec((1, 2, BAND, 2 * channels), lambda b: (b, 0, 0, 0)),
        out_shape=jax.ShapeDtypeStruct((bands, 2, BAND, 2 * channels), F32),
        compiler_params=pltpu.CompilerParams(vmem_limit_bytes=56 << 20),
    )(first, second, rows, turn)


def response_grad_kernel(lag_ref, cols_ref, turn_ref, out_ref):
    length, channels = out_ref.shape
    tile = lambda v: jnp.concatenate([v] * (channels // LANES), axis=1)
    c, s = tile(turn_ref[0]) * (1.0 / length), tile(turn_ref[1]) * (1.0 / length)
    p, q = lag_ref[:BAND], lag_ref[BAND:]
    turned = jnp.concatenate([(c * p - s * q).astype(BF), (s * p + c * q).astype(BF)], axis=0)
    step = dot_nn(cols_ref[...], turned)

    @pl.when(pl.program_id(0) == 0)
    def _():
        out_ref[...] = step

    @pl.when(pl.program_id(0) > 0)
    def _():
        out_ref[...] += step


def response_grad(lag, cols, turn):
    length = cols.shape[0]
    channels = lag.shape[1]
    return pl.pallas_call(
        response_grad_kernel,
        name="response_grad",
        grid=(length // BAND,),
        in_specs=[
            pl.BlockSpec((2 * BAND, channels), lambda b: (b, 0)),
            pl.BlockSpec((length, 2 * BAND), lambda b: (0, b)),
            pl.BlockSpec((2, BAND, LANES), lambda b: (0, b, 0)),
        ],
        out_specs=out((length, channels)),
        out_shape=jax.ShapeDtypeStruct((length, channels), F32),
        compiler_params=pltpu.CompilerParams(vmem_limit_bytes=56 << 20),
    )(lag, cols, turn)


def send_kernel(a_ref, first_ref, second_ref, first_out, second_out):
    first_out[...] = dot_nn(a_ref[...], first_ref[...]).astype(BF)
    second_out[...] = dot_nn(a_ref[...], second_ref[...]).astype(BF)


def send(a, first, second):
    length, width = a.shape
    n = first.shape[1]
    return pl.pallas_call(
        send_kernel,
        name="send",
        grid=(length // ROWS,),
        in_specs=[by_rows(width), whole((width, n)), whole((width, n))],
        out_specs=[by_rows(n), by_rows(n)],
        out_shape=[jax.ShapeDtypeStruct((length, n), BF)] * 2,
    )(a, first, second)


def join_kernel(a_ref, b_ref, add_ref, out_ref):
    out_ref[...] = (dot_nn(a_ref[...], b_ref[...]) + add_ref[...].astype(F32)).astype(BF)


def join(a, b, add):
    length, width = a.shape
    n = b.shape[1]
    return pl.pallas_call(
        join_kernel,
        name="join",
        grid=(length // ROWS,),
        in_specs=[by_rows(width), whole((width, n)), by_rows(n)],
        out_specs=by_rows(n),
        out_shape=jax.ShapeDtypeStruct((length, n), BF),
    )(a, b, add)


def before_gate_kernel(
    slot, length_ref, both_ref, mix_ref, near_ref, mix_bias_ref, normed_ref, value_ref, value_bias_ref,
    cot_ref, out_ref, part_ref, act_ref, first_ref, second_ref, up_ref, sum_ref,
):
    i = pl.program_id(0)
    part_ref[...] = dot_nn(both_ref[...], mix_ref[...]) + near_ref[...].astype(F32) + mix_bias_ref[...]
    act, slope = gelu_pair(dot_nn(normed_ref[...], value_ref[...]) + value_bias_ref[...])
    cot = cot_ref[0].astype(F32)
    time_at = lax.broadcasted_iota(jnp.int32, cot.shape, 0) + i * ROWS
    upstream = jnp.where(time_at < length_ref[slot], cot, 0.0)
    low = upstream.astype(BF)
    grad_hidden = dot_nn(low, out_ref[...])
    act_ref[...] = act
    first_ref[...] = grad_hidden * act
    second_ref[...] = grad_hidden * slope
    up_ref[...] = low

    @pl.when(i == 0)
    def _():
        sum_ref[...] = jnp.zeros_like(sum_ref)

    sum_ref[...] += jnp.sum(upstream, axis=0, keepdims=True)


def before_gate(both, mix, near, mix_bias, normed, last_all, value_bias, cotangent, lengths, slot):
    length, width = normed.shape
    n = mix.shape[1]
    return pl.pallas_call(
        functools.partial(before_gate_kernel, slot),
        name="before_gate",
        grid_spec=pltpu.PrefetchScalarGridSpec(
            num_scalar_prefetch=1,
            grid=(length // ROWS,),
            in_specs=[
                by_rows(both.shape[1]),
                whole(mix.shape),
                by_rows(n),
                whole((1, n)),
                by_rows(width),
                whole((width, n)),
                whole((1, n)),
                pl.BlockSpec((1, ROWS, width), lambda i, *at: (slot, i, 0)),
                pl.BlockSpec((width, n), lambda *at: (0, 1), pipeline_mode=pl.Buffered(1)),
            ],
            out_specs=[by_rows(n)] * 4 + [by_rows(width), out((1, width))],
        ),
        out_shape=[jax.ShapeDtypeStruct((length, n), F32)] * 4
        + [jax.ShapeDtypeStruct((length, width), BF), jax.ShapeDtypeStruct((1, width), F32)],
        compiler_params=pltpu.CompilerParams(vmem_limit_bytes=56 << 20),
    )(lengths, both, mix, near, mix_bias, normed, last_all, value_bias, cotangent, last_all)


def gate_kernel(part_ref, far_ref, act_ref, first_ref, second_ref, hidden_ref, gate_ref, value_ref, sum_ref):
    gate_act, gate_slope = gelu_pair(part_ref[...] + far_ref[...].astype(F32))
    hidden_ref[...] = (gate_act * act_ref[...]).astype(BF)
    gate = (gate_slope * first_ref[...]).astype(BF)
    value = (gate_act * second_ref[...]).astype(BF)
    gate_ref[...] = gate
    value_ref[...] = value

    @pl.when(pl.program_id(0) == 0)
    def _():
        sum_ref[...] = jnp.zeros_like(sum_ref)

    sum_ref[0:1, :] += jnp.sum(gate.astype(F32), axis=0, keepdims=True)
    sum_ref[1:2, :] += jnp.sum(value.astype(F32), axis=0, keepdims=True)


def gate(part, far, act, first, second):
    length, n = part.shape
    return pl.pallas_call(
        gate_kernel,
        name="gate",
        grid=(length // ROWS,),
        in_specs=[by_rows(n)] * 5,
        out_specs=[by_rows(n)] * 3 + [out((2, n))],
        out_shape=[jax.ShapeDtypeStruct((length, n), BF)] * 3 + [jax.ShapeDtypeStruct((2, n), F32)],
        compiler_params=pltpu.CompilerParams(vmem_limit_bytes=56 << 20),
    )(part, far, act, first, second)


def tables(length):
    odd = 2 * np.arange(length, dtype=np.int64) + 1
    angle = (odd[:, None] * odd[None, :]) % (8 * length) * (math.pi / (4 * length))
    bands = length // BAND
    both = np.stack([np.cos(angle).reshape(bands, BAND, length), np.sin(angle).reshape(bands, BAND, length)], axis=1)
    rows = both.reshape(2 * length, length)
    turn = odd * (math.pi / (4 * length))
    return rows.astype(BF), np.ascontiguousarray(rows.T).astype(BF), np.repeat(
        np.stack([np.cos(turn), np.sin(turn)])[:, :, None], LANES, axis=2
    ).astype(np.float32)

def gate_weight_kernel(lefts, count, side_ref, *refs):
    left_refs, right_refs, (give_ref, keep_ref) = refs[:lefts], refs[lefts:-2], refs[-2:]
    cols = give_ref.shape[2]
    for j in range(count):

        @pl.when(pl.program_id(0) == j)
        def _():
            pieces = right_refs[j * lefts : (j + 1) * lefts]
            total = dot_tn(left_refs[0][...], pieces[0][...])
            for left, piece in zip(left_refs[1:], pieces[1:]):
                total = total + dot_tn(left[...], piece[...])

            @pl.when(side_ref[0] == 0)
            def _():
                keep_ref[0] = total[:, :cols]
                give_ref[0] = total[:, cols:].astype(BF)

            @pl.when(side_ref[0] != 0)
            def _():
                keep_ref[0] = total[:, cols:]
                give_ref[0] = total[:, :cols].astype(BF)


def gate_weight(left, quarters, side):
    length, rows = left[0].shape
    count = len(quarters)
    cols = quarters[0][0].shape[1] // 2
    part = pl.BlockSpec((1, rows, cols), lambda j, side: (j, 0, 0))
    return pl.pallas_call(
        functools.partial(gate_weight_kernel, len(left), count),
        name="gate_weight",
        grid_spec=pltpu.PrefetchScalarGridSpec(
            num_scalar_prefetch=1,
            grid=(count,),
            in_specs=[whole((length, rows))] * len(left) + [whole((length, 2 * cols))] * (count * len(left)),
            out_specs=[part, part],
        ),
        out_shape=[
            jax.ShapeDtypeStruct((count, rows, cols), BF),
            jax.ShapeDtypeStruct((count, rows, cols), F32),
        ],
        compiler_params=pltpu.CompilerParams(vmem_limit_bytes=56 << 20),
    )(side, *left, *[piece for quarter in quarters for piece in quarter])


def row_weight_kernel(slots, side_ref, *refs):
    left_refs, right_refs, (give_ref, keep_ref) = refs[: 2 * slots], refs[2 * slots : -2], refs[-2:]
    rows = give_ref.shape[0]
    for j in range(2):

        @pl.when(pl.program_id(0) == j)
        def _():
            lefts = left_refs[j * slots : (j + 1) * slots]
            rights = right_refs[j * slots : (j + 1) * slots]
            total = dot_tn(lefts[0][...], rights[0][...])
            for left, right in zip(lefts[1:], rights[1:]):
                total = total + dot_tn(left[...], right[...])

            @pl.when(side_ref[0] == 0)
            def _():
                keep_ref[...] = total[:rows]
                give_ref[...] = total[rows:].astype(BF)

            @pl.when(side_ref[0] != 0)
            def _():
                keep_ref[...] = total[rows:]
                give_ref[...] = total[:rows].astype(BF)


def row_weight(pairs, side):
    slots = len(pairs[0][0])
    length, rows = pairs[0][0][0].shape
    cols = pairs[0][1][0].shape[1]
    part = pl.BlockSpec((rows // 2, cols), lambda j, side: (0, j))
    return pl.pallas_call(
        functools.partial(row_weight_kernel, slots),
        name="row_weight",
        grid_spec=pltpu.PrefetchScalarGridSpec(
            num_scalar_prefetch=1,
            grid=(2,),
            in_specs=[whole((length, rows))] * (2 * slots) + [whole((length, cols))] * (2 * slots),
            out_specs=[part, part],
        ),
        out_shape=[
            jax.ShapeDtypeStruct((rows // 2, 2 * cols), BF),
            jax.ShapeDtypeStruct((rows // 2, 2 * cols), F32),
        ],
        compiler_params=pltpu.CompilerParams(vmem_limit_bytes=56 << 20),
    )(side, *pairs[0][0], *pairs[1][0], *pairs[0][1], *pairs[1][1])


def conv_forward_kernel(slot, length_ref, normed_ref, weight_ref, bias_ref, rows_ref, cols_ref, k_ref, skip_ref, slope_ref, low_ref, u_ref, both_ref, total_ref):
    band = pl.program_id(0)
    length, channels = slope_ref.shape

    @pl.when(band == 0)
    def _():
        def body(i, _):
            at = pl.ds(pl.multiple_of(i * 256, 256), 256)
            pre = dot_nn(normed_ref[at, :], weight_ref[...]) + bias_ref[...]
            value, slope = gelu_pair(pre)
            time_at = lax.broadcasted_iota(jnp.int32, pre.shape, 0) + i * 256
            live = jnp.where(time_at < length_ref[slot], 1.0, 0.0)
            signal = value * live
            slope_ref[at, :] = slope * live
            low_ref[at, :] = signal.astype(BF)
            total_ref[at, :channels] = skip_ref[0:1, :] * signal
            total_ref[at, channels:] = skip_ref[1:2, :] * signal
            return 0
        lax.fori_loop(0, length // 256, body, 0)

    u = dot_nn(rows_ref[...], low_ref[...])
    u_ref[...] = u
    uc, us = u[:BAND], u[BAND:]
    k0c, k1c = k_ref[0, 0, :, :channels], k_ref[0, 0, :, channels:]
    k0s, k1s = k_ref[0, 1, :, :channels], k_ref[0, 1, :, channels:]
    product = jnp.concatenate(
        [
            jnp.concatenate([uc * k0c - us * k0s, uc * k1c + us * k1s], axis=1).astype(BF),
            jnp.concatenate([uc * k0s + us * k0c, us * k1c - uc * k1s], axis=1).astype(BF),
        ],
        axis=0,
    )
    total_ref[...] += dot_nn(cols_ref[...], product)

    @pl.when(band == pl.num_programs(0) - 1)
    def _():
        both_ref[...] = total_ref[...].astype(BF)

def conv_forward(normed, weight, bias, k, skip, lengths, rows, cols, slot):
    length, width = normed.shape
    channels = weight.shape[1]
    bands = length // BAND
    return pl.pallas_call(
        functools.partial(conv_forward_kernel, slot),
        name="conv_forward",
        grid_spec=pltpu.PrefetchScalarGridSpec(
            num_scalar_prefetch=1,
            grid=(bands,),
            in_specs=[
                whole((length, width)), whole((width, channels)), whole((1, channels)),
                pl.BlockSpec((2 * BAND, length), lambda b, n: (b, 0)),
                pl.BlockSpec((length, 2 * BAND), lambda b, n: (0, b)),
                pl.BlockSpec((1, 2, BAND, 2 * channels), lambda b, n: (b, 0, 0, 0)),
                whole((2, channels)),
            ],
            out_specs=[
                out((length, channels)), out((length, channels)),
                pl.BlockSpec((2 * BAND, channels), lambda b, n: (b, 0)),
                out((length, 2 * channels)),
            ],
            scratch_shapes=[pltpu.VMEM((length, 2 * channels), F32)],
        ),
        out_shape=[
            jax.ShapeDtypeStruct((length, channels), F32),
            jax.ShapeDtypeStruct((length, channels), BF),
            jax.ShapeDtypeStruct((2 * length, channels), F32),
            jax.ShapeDtypeStruct((length, 2 * channels), BF),
        ],
        compiler_params=pltpu.CompilerParams(vmem_limit_bytes=56 << 20),
    )(lengths, normed, weight, bias, rows, cols, k, skip)

def conv_backward_kernel(count, *refs):
    pieces, mixes = refs[:count], refs[count:2 * count]
    rows_ref, cols_ref, k_ref, u_ref, slope_ref, low_ref, skip_ref, before_ref, feed_ref, lag_ref, skips_ref, both_ref, total_ref = refs[2 * count:]
    band = pl.program_id(0)
    length, channels = slope_ref.shape

    blocks = length // ROWS

    @pl.when(band == 0)
    def _():
        skips_ref[...] = jnp.zeros_like(skips_ref)

    @pl.when(band < blocks)
    def _():
        at = pl.ds(pl.multiple_of(band * ROWS, ROWS), ROWS)
        both = dot_nt(pieces[0][...], mixes[0][...])
        for piece, mix in zip(pieces[1:], mixes[1:]):
            both = both + dot_nt(piece[...], mix[...])
        both_ref[at, :] = both.astype(BF)
        total_ref[at, :] = skip_ref[0:1, :] * both[:, :channels] + skip_ref[1:2, :] * both[:, channels:]
        signal = low_ref[...].astype(F32)
        skips_ref[...] += jnp.sum(both * jnp.concatenate([signal, signal], axis=1), axis=0, keepdims=True)

    @pl.when(band >= blocks)
    def _():
        conv_backward_band(
            rows_ref, cols_ref, k_ref, u_ref, before_ref, lag_ref, both_ref, total_ref, channels
        )

    @pl.when(band == pl.num_programs(0) - 1)
    def _():
        feed_ref[...] = (slope_ref[...] * total_ref[...]).astype(BF)


def conv_backward_band(rows_ref, cols_ref, k_ref, u_ref, before_ref, lag_ref, both_ref, total_ref, channels):
    g = dot_nn(rows_ref[...], both_ref[...])
    ac, bc = g[:BAND, :channels], g[:BAND, channels:]
    as_, bs = g[BAND:, :channels], g[BAND:, channels:]
    uc, us = u_ref[:BAND], u_ref[BAND:]
    k0c, k1c = k_ref[0, 0, :, :channels], k_ref[0, 0, :, channels:]
    k0s, k1s = k_ref[0, 1, :, :channels], k_ref[0, 1, :, channels:]
    back = jnp.concatenate(
        [
            (ac * k0c + as_ * k0s + bc * k1c - bs * k1s).astype(BF),
            (as_ * k0c - ac * k0s + bc * k1s + bs * k1c).astype(BF),
        ],
        axis=0,
    )
    if before_ref is None:
        lag_ref[:BAND, :channels] = ac * uc + as_ * us
        lag_ref[:BAND, channels:] = uc * bc + us * bs
        lag_ref[BAND:, :channels] = as_ * uc - ac * us
        lag_ref[BAND:, channels:] = us * bc - uc * bs
    else:
        lag_ref[:BAND, :channels] = before_ref[:BAND, :channels] + ac * uc + as_ * us
        lag_ref[:BAND, channels:] = before_ref[:BAND, channels:] + uc * bc + us * bs
        lag_ref[BAND:, :channels] = before_ref[BAND:, :channels] + as_ * uc - ac * us
        lag_ref[BAND:, channels:] = before_ref[BAND:, channels:] + us * bc - uc * bs
    total_ref[...] += dot_nn(cols_ref[...], back)

def conv_backward(pieces, mixes, k, u, slope, low, skip, rows, cols, before):
    length, channels = slope.shape
    width = pieces[0].shape[1]
    bands = length // BAND
    blocks = length // ROWS
    band = lambda b: jnp.maximum(b - blocks, 0)
    band_spec = pl.BlockSpec((2 * BAND, 2 * channels), lambda b: (band(b), 0))
    streamed = lambda n: pl.BlockSpec((ROWS, n), lambda b: (jnp.minimum(b, blocks - 1), 0))
    count = len(pieces)
    def kernel(*refs):
        at = 2 * count + 7
        if before is None: refs = refs[:at] + (None,) + refs[at:]
        conv_backward_kernel(count, *refs)
    return pl.pallas_call(
        kernel,
        name="conv_backward",
        grid=(blocks + bands,),
        in_specs=[streamed(width)] * count + [whole((2 * channels, width))] * count + [
            pl.BlockSpec((2 * BAND, length), lambda b: (band(b), 0)),
            pl.BlockSpec((length, 2 * BAND), lambda b: (0, band(b))),
            pl.BlockSpec((1, 2, BAND, 2 * channels), lambda b: (band(b), 0, 0, 0)),
            pl.BlockSpec((2 * BAND, channels), lambda b: (band(b), 0)),
            whole((length, channels)), streamed(channels), whole((2, channels)),
        ] + ([] if before is None else [band_spec]),
        out_specs=[out((length, channels)), band_spec, out((1, 2 * channels))],
        out_shape=[
            jax.ShapeDtypeStruct((length, channels), BF),
            jax.ShapeDtypeStruct((2 * length, 2 * channels), F32),
            jax.ShapeDtypeStruct((1, 2 * channels), F32),
        ],
        scratch_shapes=[pltpu.VMEM((length, 2 * channels), BF), pltpu.VMEM((length, channels), F32)],
        compiler_params=pltpu.CompilerParams(vmem_limit_bytes=60 << 20),
    )(*pieces, *mixes, rows, cols, k, u, slope, low, skip, *(() if before is None else (before,)))


def make_shards(dp_size, tensor_size):
    core_swap = [(i, i ^ 1) for i in range(tensor_size)]
    far_swap = [(i, i ^ 2) for i in range(tensor_size)]
    parts_of = dp_size // tensor_size

    def near(v):
        return lax.ppermute(v, "tensor", core_swap)

    def far(v):
        return lax.ppermute(v, "tensor", far_swap)

    def across(v, mask):
        return lax.ppermute(v, "dp", [(i, i ^ mask) for i in range(dp_size)])

    def shards(
        inputs,
        cotangent,
        lengths,
        norm_gain,
        norm_bias,
        value_weight,
        value_bias,
        feed_weight,
        feed_bias,
        mix_forward,
        mix_backward,
        mix_bias,
        out_weight,
        out_bias,
        state_delta,
        state_rate,
        state_readout,
        state_skip,
    ):
        slots, length, width = inputs.shape
        channels = feed_weight.shape[1]
        hidden_width = value_weight.shape[1]
        states = state_rate.shape[2]
        me = lax.axis_index("tensor")
        rank = lax.axis_index("dp")
        core = me % 2
        half = length // 2

        def collect(v):
            whole_v = v[None]
            mask = dp_size // 2
            stages = []
            while mask:
                stages.append(whole_v)
                other = across(whole_v, mask)
                upper = (rank & mask) != 0
                whole_v = jnp.stack(
                    [jnp.where(upper, other, whole_v), jnp.where(upper, whole_v, other)], axis=1
                )
                whole_v = whole_v.reshape((-1,) + v.shape)
                mask //= 2
            return whole_v.reshape((-1,) + v.shape[1:]), stages

        class Halving:
            def __init__(self, blocks):
                self.blocks = blocks
                self.give = None

            def send(self, give, keep, mask):
                self.give, self.blocks = give, keep
                self.got = across(give, mask)
                return self

            def launch(self, mask, flip=False):
                upper = ((rank & mask) != 0) ^ flip
                pairs = list(zip(self.blocks[::2], self.blocks[1::2]))
                self.give = jnp.concatenate(
                    [jnp.where(upper, a, b).astype(BF) for a, b in pairs], axis=0
                )
                self.blocks = [jnp.where(upper, b, a) for a, b in pairs]
                self.got = across(self.give, mask)
                return self

            def land(self, *anchors):
                got = after(self.got, *anchors)
                size = self.blocks[0].shape[0]
                self.blocks = [
                    b + got[i * size : (i + 1) * size].astype(F32) for i, b in enumerate(self.blocks)
                ]
                return self

        def row_blocks(v, count):
            size = v.shape[0] // count
            return [v[i * size : (i + 1) * size] for i in range(count)]

        def side(mask):
            return ((rank & mask) != 0).astype(jnp.int32).reshape(1)

        def total_over_dp(v):
            mask = 1
            while mask < dp_size:
                v = v + across(v, mask)
                mask *= 2
            return v

        feed_full, feed_stages = collect(feed_weight)
        mix_own = jnp.concatenate([mix_forward, mix_backward], axis=0)
        mix_all = lax.all_gather(mix_own, "dp", axis=0, tiled=False)
        last_own = jnp.concatenate([value_weight, out_weight.T], axis=1)
        last_all = lax.all_gather(last_own, "dp", axis=0, tiled=True)

        delta = state_delta[:, None, :]
        rate = jnp.swapaxes(state_rate, 1, 2)
        readout = jnp.swapaxes(state_readout, 1, 2)
        fourier_rows, fourier_cols, turn = (jnp.asarray(v) for v in tables(length))
        pulses = [
            impulse(after(delta, feed_stages[c - 2]), rate, readout, length, c) for c in range(2)
        ]
        spectra = response(pulses[0], pulses[1], fourier_rows, turn)

        time_at = jnp.arange(length)[:, None]
        normed, slope, low, u, both = [], [], [], [], []
        for slot in range(slots):
            rows = inputs[slot].astype(F32)
            center = rows - jnp.mean(rows, axis=-1, keepdims=True)
            spread = jnp.mean(center * center, axis=-1, keepdims=True)
            normed.append((center * lax.rsqrt(spread + EPSILON) * norm_gain + norm_bias).astype(BF))
        for slot in range(slots):
            parts = conv_forward(
                normed[slot],
                feed_full,
                feed_bias[None, :],
                spectra,
                state_skip,
                lengths,
                fourier_rows,
                fourier_cols,
                slot,
            )
            for whole_list, part in zip((slope, low, u, both), parts):
                whole_list.append(part)

        mix_all = after(mix_all, *both)
        mix_groups = mix_all.reshape((tensor_size, parts_of) + mix_own.shape)
        mix_of = []
        for j in range(tensor_size):
            quarter = lax.dynamic_index_in_dim(mix_groups, me ^ j, axis=0, keepdims=False)
            mix_of.append(jnp.concatenate([quarter[i] for i in range(parts_of)], axis=1))

        passed = None
        near_own, passes = [], []
        for slot in range(slots):
            left = both[slot] if passed is None else after(both[slot], passed)
            to_own, to_pass = send(left, mix_of[1], mix_of[3])
            passed = join(left, mix_of[2], near(to_pass))
            near_own.append(near(to_own))
            passes.append(passed)
        last_all = after(last_all, passed)
        pre = []
        for slot in range(slots):
            pre.append(
                before_gate(
                    both[slot],
                    mix_of[0],
                    near_own[slot],
                    mix_bias[None, :],
                    normed[slot],
                    last_all,
                    value_bias[None, :],
                    cotangent,
                    lengths,
                    slot,
                )
            )
        upstream_low = [p[4] for p in pre]
        value_full = last_all[:, :hidden_width]
        out_all = last_all[:, hidden_width:]

        hidden, grad_gate, grad_value, gate_sums = [], [], [], []
        for slot in range(slots):
            arrived = far(passes[slot])
            if slot == 0:
                arrived = after(arrived, pre[-1][0])
            else:
                arrived = after(arrived, grad_gate[-1])
            parts = gate(pre[slot][0], arrived, *pre[slot][1:4])
            for whole_list, part in zip((hidden, grad_gate, grad_value, gate_sums), parts):
                whole_list.append(part)
        far_gate = [far(g) for g in grad_gate]
        near_gate = [near(g) for g in grad_gate]

        top = dp_size // 2
        give, keep = row_weight(((normed, grad_value), (upstream_low, hidden)), side(top))
        last_sum = Halving(None).send(give, [keep], top)

        def next_rows(halving, mask, *anchors):
            halving.land(*anchors)
            halving.blocks = row_blocks(halving.blocks[0], 2)
            return halving.launch(mask)

        first = core == 0
        branches = [dot_nt(hidden[slot], out_all) for slot in range(slots)]
        branch_keep = jnp.where(first, branches[0], branches[1])
        branch_give = jnp.where(first, branches[1], branches[0]).astype(BF)

        low_masks = [1 << i for i in range(parts_of.bit_length() - 1)]

        def start_low(quarters):
            quarters = [[after(piece, last_sum.give) for piece in quarter] for quarter in quarters]
            if parts_of == 2:
                give, keep = gate_weight(both, quarters, side(1))
                return Halving(None).send(give.reshape(-1, give.shape[2]), [keep[0], keep[1]], 1)
            size = hidden_width // parts_of
            blocks = []
            for quarter in quarters:
                g = sum(dot_tn(b, piece) for b, piece in zip(both, quarter))
                blocks += [g[:, i * size : (i + 1) * size] for i in range(parts_of)]
            return Halving(blocks).launch(low_masks[0])

        def finish_low(halving, *anchors):
            for mask in low_masks[1:]:
                halving.land(*anchors).launch(mask)
            return halving.land(*anchors).launch(parts_of, core == 1)

        near_sum = start_low([grad_gate, near_gate])
        branch_pair = (branch_keep + near(branch_give).astype(F32)).astype(BF)

        early = [sum(g[0:1] for g in gate_sums), sum(g[1:2] for g in gate_sums), sum(p[5] for p in pre)]

        def back(slot, arrived, lag, *anchors):
            pieces = [grad_gate[slot], near_gate[slot], arrived, near(arrived)]
            pieces[0] = after(pieces[0], *anchors)
            return pieces[3], conv_backward(
                pieces,
                mix_of,
                spectra,
                u[slot],
                slope[slot],
                low[slot],
                state_skip,
                fourier_rows,
                fourier_cols,
                lag,
            )

        def features(slot, grad_feed):
            v = dot_nt(grad_value[slot], value_full) + dot_nt(grad_feed, feed_full)
            give = lax.dynamic_slice_in_dim(v, (1 - core) * half, half, 0).astype(BF)
            keep = lax.dynamic_slice_in_dim(v, core * half, half, 0)
            return give, keep

        arrived_a = after(far_gate[0], last_sum.give)
        far_near_a, (grad_feed_a, lag, skips_a) = back(
            0, arrived_a, None, near_sum.give, last_sum.give, branch_pair
        )
        give_a, keep_a = features(0, grad_feed_a)
        near_a = near(give_a)
        masks = [top >> i for i in range(1, top.bit_length())]
        next_rows(last_sum, masks[0], grad_feed_a)
        near_sum = finish_low(near_sum, grad_feed_a)

        arrived_b = after(far_gate[1], last_sum.give, near_sum.give, give_a)
        far_near_b = near(arrived_b)
        far_sum = start_low([[arrived_a, arrived_b], [far_near_a, far_near_b]])
        pair_a = (keep_a + near_a.astype(F32)).astype(BF)
        far_near_b, (grad_feed_b, lag, skips_b) = back(1, arrived_b, lag, far_sum.give, pair_a)
        far_a = far(pair_a)
        for mask in masks[1:]:
            next_rows(last_sum, mask, grad_feed_b)
        give_b, keep_b = features(1, grad_feed_b)
        near_b = near(give_b)
        near_sum.land(grad_feed_b)
        far_sum = finish_low(far_sum, give_b)

        feed_sum = Halving(
            row_blocks(dot_tn(normed[0], grad_feed_a) + dot_tn(normed[1], grad_feed_b), 2)
        ).launch(top)
        feed_bias_sum = jnp.sum(grad_feed_a.astype(F32), axis=0, keepdims=True) + jnp.sum(
            grad_feed_b.astype(F32), axis=0, keepdims=True
        )
        grad_response = response_grad(after(lag, give_b, far_sum.give, feed_sum.give), fourier_cols, turn)
        pair_b = (keep_b + after(near_b, grad_response).astype(F32)).astype(BF)
        far_b = far(pair_b)

        def state_step(c, *anchors):
            at = slice(c * channels, (c + 1) * channels)
            extra = [skips_a[:, at], skips_a[:, at] + skips_b[:, at]] + [v[:, at] for v in early]
            extra += [feed_bias_sum] * 3
            return state_grad(
                delta, rate, readout, after(grad_response, *anchors), jnp.concatenate(extra, axis=0), c
            )

        def finish_rows(slot, pair, arrived):
            total = pair.astype(F32) + arrived.astype(F32)
            rows = lax.dynamic_slice_in_dim(inputs[slot], core * half, half, 0).astype(F32)
            up_half = lax.dynamic_slice_in_dim(upstream_low[slot], core * half, half, 0).astype(F32)
            center = rows - jnp.mean(rows, axis=-1, keepdims=True)
            spread = jnp.mean(center * center, axis=-1, keepdims=True)
            inverse = lax.rsqrt(spread + EPSILON)
            unit = center * inverse
            weighted = total * norm_gain
            mine = (
                up_half
                + (
                    weighted
                    - jnp.mean(weighted, axis=-1, keepdims=True)
                    - unit * jnp.mean(weighted * unit, axis=-1, keepdims=True)
                )
                * inverse
            ).astype(BF)
            sums = jnp.concatenate(
                [jnp.sum(total * unit, axis=0, keepdims=True), jnp.sum(total, axis=0, keepdims=True)], axis=0
            )
            return mine, sums

        masks_up = [1 << i for i in range(dp_size.bit_length() - 1)]
        state_a = state_step(0, pair_b)
        sent = across(state_a, masks_up[0])
        far_sum.land(state_a)
        mix_sum = Halving([near_sum.blocks[0], far_sum.blocks[0]]).launch(2 * parts_of, me >= 2)
        next_rows(feed_sum, masks[0], state_a)

        rows = jnp.where(first, inputs[0], inputs[1]).astype(F32)
        live = (time_at < jnp.where(first, lengths[0], lengths[1])).astype(F32)
        branch_far = after(far(branch_pair), state_a)
        mine = (live * (rows + (branch_pair.astype(F32) + branch_far.astype(F32)) + out_bias)).astype(BF)
        theirs = near(mine)
        rows_a, norm_a = finish_rows(0, pair_a, after(far_a, state_a))
        state_a = state_a + after(sent, rows_a, mine)
        sent = across(state_a, masks_up[1])
        state_b = state_step(1, state_a, mix_sum.give, feed_sum.give, theirs)
        layer_out = jnp.stack([jnp.where(first, mine, theirs), jnp.where(first, theirs, mine)])
        state_a = state_a + after(sent, state_b)
        sent_b = across(state_b, masks_up[0])
        for mask in masks_up[2:]:
            sent = across(state_a, mask)
            state_a = state_a + (after(sent, layer_out) if mask < top else sent)
        rows_b, norm_b = finish_rows(1, pair_b, after(far_b, state_b))
        mine = jnp.stack([rows_a, rows_b])
        theirs = near(mine)
        state_b = state_b + after(sent_b, rows_b)
        sent_b = across(state_b, masks_up[1])
        for i, mask in enumerate(masks[1:]):
            next_rows(feed_sum, mask, *((rows_b,) if i == 0 else ()))
        small = after(norm_a + norm_b, state_b)
        small_sent = across(small, masks_up[0])
        last_sum = last_sum.land(state_b).blocks[0]
        state_b = state_b + after(sent_b, last_sum)
        sent_b = across(state_b, masks_up[2])
        small = small + after(small_sent, state_b)
        small_sent = across(small, masks_up[1])
        mix_sum = mix_sum.land(state_b).blocks[0]
        theirs = after(theirs, mix_sum)
        input_grad = jnp.concatenate([jnp.where(first, mine, theirs), jnp.where(first, theirs, mine)], axis=1)
        small = small + after(small_sent, mix_sum)
        small_sent = across(small, masks_up[2])
        feed_sum = feed_sum.land(mix_sum).blocks[0]
        state_b = state_b + after(sent_b, input_grad)
        small = small + small_sent
        for mask in masks_up[3:]:
            state_b = state_b + across(state_b, mask)
            small = small + across(small, mask)
        norm_sums = small + near(small)
        totals = jnp.stack([state_a, state_b])
        tail_rows = totals[:, 2 * states :]
        early = [tail_rows[:, i].reshape(-1) for i in (2, 3, 4)]

        return (
            layer_out,
            input_grad,
            norm_sums[0],
            norm_sums[1],
            last_sum[:, :hidden_width],
            early[1],
            feed_sum,
            tail_rows[0, 5],
            mix_sum[:channels],
            mix_sum[channels:],
            early[0],
            last_sum[:, hidden_width:].T,
            early[2],
            tail_rows[:, 0],
            jnp.swapaxes(totals[:, :states], 1, 2),
            jnp.swapaxes(totals[:, states : 2 * states], 1, 2),
            tail_rows[:, 1],
        )

    return shards


def solution(mesh):
    placed = (
        P("dp", None, None),
        P("dp", None, None),
        P("dp"),
        P(),
        P(),
        P("dp", "tensor"),
        P("tensor"),
        P("dp", "tensor"),
        P("tensor"),
        P("tensor", "dp"),
        P("tensor", "dp"),
        P("tensor"),
        P("tensor", "dp"),
        P(),
        P(None, "tensor"),
        P(None, "tensor", None),
        P(None, "tensor", None),
        P(None, "tensor"),
    )
    return jax.shard_map(
        make_shards(mesh.shape["dp"], mesh.shape["tensor"]),
        mesh=mesh,
        in_specs=placed,
        out_specs=(
            P("dp", None, None),
            P("dp", None, None),
            P(),
            P(),
            P("dp", "tensor"),
            P("tensor"),
            P("dp", "tensor"),
            P("tensor"),
            P("tensor", "dp"),
            P("tensor", "dp"),
            P("tensor"),
            P("tensor", "dp"),
            P(),
            P(None, "tensor"),
            P(None, "tensor", None),
            P(None, "tensor", None),
            P(None, "tensor"),
        ),
        check_vma=False,
    )
```
